256 devices in a mesh: rows: 256 (over x, y, z, core).
Axes of the slice: x: 4, y: 4, z: 8, core: 2. Of those that a mesh axis runs over, the one named last changes fastest.
Arguments:
- density: float32 [1024, 64, 512], P('rows'), may hold values from -0.75 to 0.75
- send_rows: int32 [256, 13, 2], replicated, may hold values from -1 to 3, as said below
- recv_pos: int32 [1024, 3], replicated, may hold values from 0 to 25, as said below
Outputs:
- purified: float32 [1024, 64, 512], P('rows')
The draws below stay inside these ranges and needn't reach their ends.
Inputs may be any that keep to these rules, and one draw needn't show every extreme that they name: `send_rows`: entry (d, g, p) is the local block row that device d sends in slot p of its group-g message, to the device at loop position (d - o_g) mod the number of devices; -1 marks an empty slot. Used slots come first, hold distinct rows and number 1 to 2 in a message; some message of every draw uses all 2. `recv_pos`: entry (r, e) = g * 2 + p names a used slot p of the group-g message that the owner of block row r receives; the block row carried there is the column of r's e-th out-of-band block. The 3 entries of a row are distinct.
All inputs are finite; a program needn't handle non-finite values.
Results may differ from the reference program's by a relative error of at most 0.0003.
Values sent between devices are 32-bit elements; how exact they have to be, the bound alone decides.
A program may use at most 64 MiB of HBM per device.

```python
import jax
import jax.numpy as jnp
from jax import lax

B = 64
H = 2
E = 3
NS = 8
BR_DEV = 4
CAP = 2
G = 13
NBR = 1024
N_ROWS = 256


def offsets_table():
    levels = (G + 3) // 2
    forward = [2 ** (position + 1) for position in range(levels - 1)]
    backward = [-2 ** (position + 1) for position in range(levels - 2)]
    return jnp.array(forward + backward, dtype=jnp.int32)


def pattern_lists(key):
    total_rows = BR_DEV * N_ROWS
    counts = jax.random.randint(jax.random.fold_in(key, 11), (N_ROWS, G), 1, CAP + 1, dtype=jnp.int32)
    hot_device = jax.random.randint(jax.random.fold_in(key, 12), (), 0, N_ROWS, dtype=jnp.int32)
    hot_group = jax.random.randint(jax.random.fold_in(key, 13), (), 0, G, dtype=jnp.int32)
    device_axis = jnp.arange(N_ROWS, dtype=jnp.int32)[:, None]
    group_axis = jnp.arange(G, dtype=jnp.int32)[None, :]
    counts = jnp.where((device_axis == hot_device) & (group_axis == hot_group), CAP, counts).astype(jnp.int32)
    scores = jax.random.randint(jax.random.fold_in(key, 14), (N_ROWS, G, BR_DEV), 0, 1 << 16, dtype=jnp.int32) * BR_DEV + jnp.arange(BR_DEV, dtype=jnp.int32)
    chosen = jnp.argsort(scores, axis=-1, stable=True)[:, :, :CAP].astype(jnp.int32)
    send_table = jnp.where(jnp.arange(CAP, dtype=jnp.int32)[None, None, :] < counts[:, :, None], chosen, -1).astype(jnp.int32)
    owners = jnp.arange(total_rows, dtype=jnp.int32) // BR_DEV
    senders = (owners[:, None] + offsets_table()[None, :]) % N_ROWS
    usable = jnp.arange(CAP, dtype=jnp.int32)[None, None, :] < counts[senders, group_axis][:, :, None]
    keys_draw = jax.random.randint(jax.random.fold_in(key, 15), (total_rows, G * CAP), 0, 1 << 16, dtype=jnp.int32) * (G * CAP) + jnp.arange(G * CAP, dtype=jnp.int32)
    keys_draw = keys_draw + jnp.where(usable.reshape(total_rows, G * CAP), 0, 1 << 29).astype(jnp.int32)
    recv_table = jnp.argsort(keys_draw, axis=-1, stable=True)[:, :E].astype(jnp.int32)
    return (send_table, recv_table)


def draw_send_rows(key, part):
    return pattern_lists(key)[0]


def draw_recv_pos(key, part):
    return pattern_lists(key)[1]


def shard_levels(key, dims, cuts, least, top_value):
    gain, own = 1.0, jax.random.fold_in(key, 6)
    for dim, shards_of in cuts:
        draws = jnp.exp(jax.random.uniform(jax.random.fold_in(own, dim), (shards_of,), jnp.float32, least / len(cuts), top_value / len(cuts)))
        gain = gain * jnp.repeat(draws, dims[dim] // shards_of).reshape([-1 if axis == dim else 1 for axis in range(len(dims))])
    return gain


def centred(rng, shape, width, reach, split=(), kind=jnp.bfloat16):
    values = width * jax.random.normal(rng, shape, jnp.float32)
    if split:
        values = values * shard_levels(rng, shape, split, -0.22, 0.18)
    return jnp.clip(values, -reach, reach).astype(kind)


def setup_inputs(seed: int = 0) -> dict:
    streams_of = jax.random.split(jax.random.key(seed), 4)
    return {
        "density": centred(streams_of[0], (NBR, B, NS * B), 0.12, 0.75, ((0, 256),), jnp.float32),
        "send_rows": draw_send_rows(jax.random.fold_in(streams_of[3], 71), 0),
        "recv_pos": draw_recv_pos(jax.random.fold_in(streams_of[3], 71), 0),
    }


def offset_list(count_dev):
    levels = count_dev.bit_length() - 1
    forward = [2 ** (position + 1) for position in range(levels - 1)]
    backward = [-(2 ** (position + 1)) for position in range(levels - 2)]
    return forward + backward


def column_table(send_rows, recv_pos, per_dev, count_dev, shifts_by, half_band, slots_cap):
    total_rows = per_dev * count_dev
    offset_values = jnp.array(shifts_by, dtype=jnp.int32)
    global_rows = jnp.arange(total_rows, dtype=jnp.int32)
    owners = global_rows // per_dev
    groups_of = (recv_pos // slots_cap).astype(jnp.int32)
    places = (recv_pos % slots_cap).astype(jnp.int32)
    senders = ((owners[:, None] + offset_values[groups_of]) % count_dev).astype(jnp.int32)
    local_rows = send_rows[senders, groups_of, places]
    far_cols = senders * per_dev + local_rows
    band_cols = (global_rows[:, None] + jnp.arange(-half_band, half_band + 1, dtype=jnp.int32)[None, :]) % total_rows
    return jnp.concatenate([band_cols, far_cols], axis=1).astype(jnp.int32)


def row_product(left_panel, right_rows, columns, row_index):
    own_cols = columns[row_index]
    picked = right_rows[own_cols]
    picked_cols = columns[own_cols]
    matches = (picked_cols[:, :, None] == own_cols[None, None, :]).astype(jnp.float32)
    slot_count = own_cols.shape[0]
    block_width = picked.shape[1]
    tiles_view = picked.reshape(slot_count, block_width, slot_count, block_width)
    gathered = jnp.einsum("sut,saub->satb", matches, tiles_view, precision=lax.Precision.HIGHEST)
    gathered = gathered.reshape(slot_count * block_width, slot_count * block_width)
    return jnp.dot(left_panel, gathered, precision=lax.Precision.HIGHEST, preferred_element_type=jnp.float32)


def reference(density, send_rows, recv_pos):
    shifts_by = offset_list(N_ROWS)
    columns = column_table(send_rows, recv_pos, BR_DEV, N_ROWS, shifts_by, H, CAP)
    rows_all = jnp.arange(BR_DEV * N_ROWS, dtype=jnp.int32)
    square = lax.map(lambda row_index: row_product(density[row_index], density, columns, row_index), rows_all)
    cube_rows = lax.map(lambda row_index: row_product(square[row_index], density, columns, row_index), rows_all)
    return 3.0 * square - 2.0 * cube_rows
```

```python
import functools

import jax
import jax.numpy as jnp
from jax import lax
from jax.experimental import pallas as pl
from jax.experimental.pallas import tpu as pltpu
from jax.sharding import PartitionSpec as P

MESH = pl.DeviceIdType.MESH
B = 64
ORDER = (2, 9, 1, 8, 0, 7, 3, 10, 4, 11, 5, 12, 6)
PANELS = 5


def offset_list(count_dev):
    levels = count_dev.bit_length() - 1
    forward = [2 ** (position + 1) for position in range(levels - 1)]
    backward = [-(2 ** (position + 1)) for position in range(levels - 2)]
    return forward + backward


def flag(condition):
    return jnp.where(condition, 1.0, 0.0).astype(jnp.float32)


def kernel(
    n, offs, x_hbm, sr, rp, out,
    own, left, right, pack, recv, gh, gl, sband, table,
    own_sem, send_sem, recv_sem, halo_send, halo_recv,
):
    me = lax.axis_index("rows")
    rows = n * 4

    def device(step):
        return {"rows": lax.rem(me + step + n, n)}

    barrier = pltpu.get_barrier_semaphore()
    partners = sorted(set(offs) | set(-o for o in offs if o * 2 != n) | {1, -1})
    for step in partners:
        pl.semaphore_signal(barrier, inc=1, device_id=device(step), device_id_type=MESH)

    loads = [
        pltpu.make_async_copy(x_hbm.at[:, :, pl.ds(128 * j, 128)], own.at[j], own_sem.at[j])
        for j in range(4)
    ]
    for load in loads:
        load.start()
    for index, value in enumerate(offs):
        table[index] = value
    lane = lax.broadcasted_iota(jnp.int32, (B, 128), 1)
    low = lane < B
    for load in loads:
        load.wait()

    def tile(k, j):
        if k < 2:
            return left[j, k]
        return right[j, k - 6] if k > 5 else own[j, k - 2]

    def turn(panel):
        return pltpu.roll(panel, B, 1)

    def pack_group(g, carry):
        first = jnp.maximum(sr[g, 0, me], 0)
        second = jnp.maximum(sr[g, 1, me], 0)
        for slot, row in enumerate((first, second)):
            pack[g, 2 * slot] = jnp.where(low, own[1, row], own[2, row])
            pack[g, 2 * slot + 1] = own[3, row]
        delta = jnp.clip(second - first, -2, 2)
        one = own[jnp.where(delta >= 2, 2, jnp.where(delta == 1, 1, 0)), first]
        two = own[jnp.where(delta <= -2, 2, jnp.where(delta == -1, 1, 0)), second]
        odd = flag(jnp.abs(delta) == 1)
        even = 1.0 - odd
        pack[g, 4] = jnp.where(low, odd * turn(one) + even * one, odd * two + even * turn(two))
        return carry

    lax.fori_loop(0, len(offs), pack_group, 0)
    pl.semaphore_wait(barrier, len(partners))

    copies = []
    for g in ORDER:
        copies.append(pltpu.make_async_remote_copy(
            src_ref=pack.at[g], dst_ref=recv.at[pl.ds(g * PANELS, PANELS)],
            send_sem=send_sem.at[g], recv_sem=recv_sem.at[g],
            device_id=device(-offs[g]), device_id_type=MESH,
        ))
    pieces = (
        (1, own.at[pl.ds(1, 2), pl.ds(2, 2)], left.at[pl.ds(1, 2)]),
        (1, own.at[0, 3], left.at[0, 1]),
        (-1, own.at[pl.ds(0, 2), pl.ds(0, 2)], right),
    )
    halo = [
        pltpu.make_async_remote_copy(
            src_ref=source, dst_ref=target, send_sem=halo_send.at[index], recv_sem=halo_recv.at[index],
            device_id=device(step), device_id_type=MESH,
        )
        for index, (step, source, target) in enumerate(pieces)
    ]
    for copy in halo + copies:
        copy.start()

    def far_id(row, e):
        where = rp[e, row]
        group = lax.div(where, 2)
        sender = (lax.div(row, 4) + table[group] + n) % n
        return sender * 4 + jnp.maximum(sr[group, where - 2 * group, sender], 0)

    def split(value):
        high = value.astype(jnp.bfloat16)
        return high, (value - high.astype(jnp.float32)).astype(jnp.bfloat16)

    def put(i, s, j, value):
        high, rest = split(value)
        gh[i, pl.ds(s * B, B), pl.ds(j * 128, 128)] = high
        gl[i, pl.ds(s * B, B), pl.ds(j * 128, 128)] = rest

    def product(left, right_high, right_rest):
        high, rest = split(left)
        both = jnp.concatenate([high, rest], axis=0)
        wide = jnp.dot(both, right_high, preferred_element_type=jnp.float32)
        return wide[:B] + wide[B:] + jnp.dot(high, right_rest, preferred_element_type=jnp.float32)

    zero = jnp.zeros((B, 128), jnp.float32)

    def halves(first, second):
        return jnp.where(low, first, second)

    for copy in halo:
        copy.wait()

    def narrow(i, first):
        return jnp.concatenate([own[first, i], own[first + 1, i]], axis=1)

    ids = [[far_id(me * 4 + i, e) for e in range(3)] for i in range(4)]
    for i in range(4):
        for s in range(5):
            k = i + s
            if s == 2:
                for j in range(4):
                    put(i, s, j, own[j, i])
                continue
            fourth = zero
            if s == 0:
                put(i, s, 0, tile(k, 1))
                put(i, s, 1, halves(tile(k, 2), zero))
            elif s == 1:
                r0, r1, r2 = turn(tile(k, 0)), turn(tile(k, 1)), turn(tile(k, 2))
                put(i, s, 0, halves(r0, r1))
                put(i, s, 1, halves(r1, r2))
            elif s == 3:
                r0, r1 = turn(tile(k, 0)), turn(tile(k, 1))
                put(i, s, 0, halves(zero, r0))
                put(i, s, 1, halves(r0, r1))
                fourth = r1
            else:
                put(i, s, 0, zero)
                put(i, s, 1, tile(k, 0))
                fourth = tile(k, 1)
            if k < 2 or k > 5:
                put(i, s, 2, halves(fourth, zero))
                put(i, s, 3, zero)
                continue
            meet = [[flag(ids[i][e] == ids[k - 2][f]) for f in range(3)] for e in range(3)]
            f2, f3 = tile(k, 2), tile(k, 3)
            g2, g3 = turn(f2), turn(f3)
            put(i, s, 2, halves(fourth, meet[0][0] * f2 + meet[0][1] * g3 + meet[0][2] * f3))
            put(i, s, 3, halves(
                meet[1][0] * g2 + meet[1][1] * f3 + meet[1][2] * g3,
                meet[2][0] * f2 + meet[2][1] * g3 + meet[2][2] * f3,
            ))
        sband[i] = product(narrow(i, 0), gh[i, pl.ds(0, 256), :], gl[i, pl.ds(0, 256), :])

    for copy in copies:
        copy.wait()

    def far_row(i, carry):
        row = me * 4 + i
        mine = [far_id(row, e) for e in range(3)]
        slots = [rp[e, row] for e in range(3)]
        groups = [lax.div(slot, 2) for slot in slots]
        columns = [(row - 2 + t + rows) % rows for t in range(5)] + mine
        for e in range(3):
            place = slots[e] - 2 * groups[e]
            theirs = [far_id(mine[e], f) for f in range(3)]
            start = groups[e] * PANELS
            a, b, c = recv[start + 2 * place], recv[start + 2 * place + 1], recv[start + 4]
            ra, rb, rc = turn(a), turn(b), turn(c)
            for j in range(4):
                parts = []
                for half in range(2):
                    t = 2 * j + half
                    far = [flag(column == columns[t]) for column in theirs]
                    weight = [0.0, far[0], far[1], far[2], 0.0, 0.0]
                    if half == 1:
                        weight = [far[0], 0.0, far[2], far[1], 0.0, 0.0]
                    if t >= 5:
                        if t - 5 == e:
                            weight[half] = 1.0
                        else:
                            distance = jnp.abs(mine[t - 5] - mine[e])
                            cross = jnp.logical_and(groups[t - 5] == groups[e], distance <= 2)
                            weight[4] = flag(jnp.logical_and(cross, place == half))
                            weight[5] = flag(jnp.logical_and(cross, place != half))
                    parts.append(weight)
                value = zero
                for source, left, right in zip((a, ra, b, rb, c, rc), parts[0], parts[1]):
                    if isinstance(left, float) and isinstance(right, float) and left == right == 0.0:
                        continue
                    value = value + halves(jnp.full((B, 128), left), jnp.full((B, 128), right)) * source
                put(i, 5 + e, j, value)
        square = sband[i] + product(
            narrow(i, 2), gh[i, pl.ds(256, 256), :], gl[i, pl.ds(256, 256), :]
        )
        out[i] = 3.0 * square - 2.0 * product(square, gh[i], gl[i])
        return carry

    lax.fori_loop(0, 4, far_row, 0)


def shards(density, send_rows, recv_pos):
    n = lax.axis_size("rows")
    offs = offset_list(n)
    groups = len(offs)
    dma = pltpu.SemaphoreType.DMA
    return pl.pallas_call(
        functools.partial(kernel, n, offs),
        out_shape=jax.ShapeDtypeStruct(density.shape, jnp.float32),
        in_specs=[
            pl.BlockSpec(memory_space=pl.ANY),
            pl.BlockSpec(memory_space=pltpu.SMEM),
            pl.BlockSpec(memory_space=pltpu.SMEM),
        ],
        out_specs=pl.BlockSpec(memory_space=pltpu.VMEM),
        scratch_shapes=[
            pltpu.VMEM((4, 4, B, 128), jnp.float32),
            pltpu.VMEM((3, 2, B, 128), jnp.float32),
            pltpu.VMEM((2, 2, B, 128), jnp.float32),
            pltpu.VMEM((groups, PANELS, B, 128), jnp.float32),
            pltpu.VMEM((groups * PANELS, B, 128), jnp.float32),
            pltpu.VMEM((4, 512, 512), jnp.bfloat16),
            pltpu.VMEM((4, 512, 512), jnp.bfloat16),
            pltpu.VMEM((4, B, 512), jnp.float32),
            pltpu.SMEM((16,), jnp.int32),
            dma((4,)), dma((groups,)), dma((groups,)), dma((3,)), dma((3,)),
        ],
        compiler_params=pltpu.CompilerParams(collective_id=0, has_side_effects=True),
    )(density, jnp.transpose(send_rows, (1, 2, 0)), jnp.transpose(recv_pos, (1, 0)))


def solution(mesh):
    return jax.shard_map(
        shards,
        mesh=mesh,
        in_specs=(P("rows", None, None), P(), P()),
        out_specs=P("rows", None, None),
        check_vma=False,
    )
```

```python
import functools

import jax
import jax.numpy as jnp
from jax import lax
from jax.experimental import pallas as pl
from jax.experimental.pallas import tpu as pltpu
from jax.sharding import PartitionSpec as P

MESH = pl.DeviceIdType.MESH
B = 64
ORDER = (6, 12, 5, 11, 4, 10, 3, 7, 0, 8, 1, 9, 2)
ROOMS = (4, 6, 8)


def offset_list(count_dev):
    levels = count_dev.bit_length() - 1
    forward = [2 ** (position + 1) for position in range(levels - 1)]
    backward = [-(2 ** (position + 1)) for position in range(levels - 2)]
    return forward + backward


def flag(condition):
    return jnp.where(condition, 1.0, 0.0).astype(jnp.float32)


def plan_kernel(n, offs, rp, sr, table, level):
    me = lax.axis_index("rows")
    lanes = rp.shape[1]
    per = lanes // n
    row_lane = lax.broadcasted_iota(jnp.int32, (8, lanes), 1) & (per - 1)
    lists = jnp.concatenate([rp[...], jnp.zeros((5, lanes), jnp.int32)], axis=0).astype(jnp.float32)
    spread = jnp.concatenate(
        [jnp.where(row_lane == i, lists, 0.0) for i in range(per)], axis=0
    ).astype(jnp.bfloat16)
    fold = jnp.where(
        lax.broadcasted_iota(jnp.int32, (lanes, n), 0) // per == lax.broadcasted_iota(jnp.int32, (lanes, n), 1),
        1.0, 0.0,
    ).astype(jnp.bfloat16)
    picks = jnp.dot(spread, fold, preferred_element_type=jnp.float32).astype(jnp.int32)

    lane = lax.broadcasted_iota(jnp.int32, (8, n), 1)
    sub = lax.broadcasted_iota(jnp.int32, (8, n), 0)
    small_lane = lax.broadcasted_iota(jnp.int32, (8, 128), 1)
    small_sub = lax.broadcasted_iota(jnp.int32, (8, 128), 0)

    def spread_row(value, row):
        return jnp.broadcast_to(value[row:row + 1], (8, n))

    sent, bases = [], []
    for g, off in enumerate(offs):
        turned = pltpu.roll(jnp.concatenate([jnp.maximum(sr[g], 0)] * 4, axis=0), (-off) % n, 1)
        sent.append([spread_row(turned, p) for p in range(2)])
        bases.append(((lane + (off + n)) & (n - 1)) * per)
    blocks = [picks[8 * i:8 * i + 8] for i in range(per)]
    ids = [jnp.zeros((8, n), jnp.int32) for _ in range(per)]
    for g in range(len(offs)):
        for p in range(2):
            name = bases[g] + sent[g][p]
            ids = [jnp.where(block == 2 * g + p, name, known) for block, known in zip(blocks, ids)]
    pick_rows = [[spread_row(blocks[i], e) for e in range(3)] for i in range(per)]
    id_rows = [[spread_row(ids[i], e) for e in range(3)] for i in range(per)]
    all_ids = jnp.concatenate(ids, axis=0)

    most = jnp.zeros((8, n), jnp.int32)
    for g, off in enumerate(offs):
        moved = pltpu.roll(all_ids, (-off) % n, 1)
        needs = []
        picked = [[
            (pick_rows[i][0] == 2 * g + p) | (pick_rows[i][1] == 2 * g + p) | (pick_rows[i][2] == 2 * g + p)
            for p in range(2)
        ] for i in range(per)]
        for p in range(2):
            far = moved[0:8]
            for i in range(1, per):
                far = jnp.where(sent[g][p] == i, moved[8 * i:8 * i + 8], far)
            need = None
            for i in range(per):
                meets = ((far - (lane * per + (i - 2))) & (lanes - 1)) <= 4
                for e in range(3):
                    meets = meets | (far == id_rows[i][e])
                term = picked[i][p] & meets
                need = term if need is None else need | term
            needs.append(jnp.where(need, 1, 0))
        delta = sent[g][1] - sent[g][0]
        pair = picked[0][0] & picked[0][1]
        for i in range(1, per):
            pair = pair | (picked[i][0] & picked[i][1])
        cross = jnp.where(pair & (jnp.abs(delta) <= 2), 1, 0)
        need = jnp.where(sub < 3, needs[0], jnp.where(sub < 6, pltpu.roll(needs[1], 3, 0), cross))
        rank = need
        for step in (1, 2, 4):
            rank = rank + jnp.where(sub >= step, pltpu.roll(rank, step, 0), 0)
        most = jnp.maximum(most, rank)
        rank = rank - need
        local = jnp.where((sub < 3) | (sub == 6), sent[g][0], sent[g][1])
        which = jnp.where(sub < 3, sub + 5, jnp.where(sub < 6, sub + 2, jnp.where(sub == 6, 2 + delta, 2 - delta)))
        code = (which & 1) * 16 + (which >> 1) * 4 + local
        mine = jnp.sum(jnp.where(lane == me, rank, 0), axis=1, keepdims=True)
        table[pl.ds(16 + g, 1), :] = jnp.sum(
            jnp.where(small_lane == small_sub, mine, 0), axis=0, keepdims=True
        )
        packed = jnp.where(need == 1, rank * 32 + code, 8 * 32)
        target = (me - off + n) & (n - 1)
        theirs = jnp.sum(jnp.where(lane == target, packed, 0), axis=1, keepdims=True)
        table[pl.ds(g, 1), :] = jnp.sum(
            jnp.where(small_lane == (theirs >> 5), theirs & 31, 0), axis=0, keepdims=True
        )
    biggest = jnp.max(most)
    level[0] = sum(jnp.where(biggest > room, 1, 0) for room in ROOMS[:-1])


def kernel(
    n, offs, room, x_hbm, sr, rp, table, out,
    own, left, right, pack, recv, gh, gl, sband, jumps,
    own_sem, send_sem, recv_sem, halo_send, halo_recv,
):
    me = lax.axis_index("rows")
    rows = n * 4
    panels = 1 + room // 2

    def device(step):
        return {"rows": lax.rem(me + step + n, n)}

    barrier = pltpu.get_barrier_semaphore()
    partners = sorted(set(offs) | set(-o for o in offs if o * 2 != n) | {1, -1})
    for step in partners:
        pl.semaphore_signal(barrier, inc=1, device_id=device(step), device_id_type=MESH)

    loads = [
        pltpu.make_async_copy(x_hbm.at[:, :, pl.ds(128 * j, 128)], own.at[pl.ds(4 * j, 4)], own_sem.at[j])
        for j in range(4)
    ]
    for load in loads:
        load.start()
    for index, value in enumerate(offs):
        jumps[index] = value
    lane = lax.broadcasted_iota(jnp.int32, (B, 128), 1)
    low = lane < B
    for load in loads:
        load.wait()

    def tile(k, j):
        if k < 2:
            return left[j, k]
        return right[j, k - 6] if k > 5 else own[4 * j + k - 2]

    def turn(panel):
        return pltpu.roll(panel, B, 1)

    zero = jnp.zeros((B, 128), jnp.float32)

    def halves(first, second):
        return jnp.where(low, first, second)

    def pack_group(g, carry):
        first = jnp.maximum(sr[g, 0, me], 0)
        second = jnp.maximum(sr[g, 1, me], 0)
        pack[g, 0] = halves(own[4 + first], turn(own[4 + second]))
        for c in range(0, room, 2):
            one, two = table[g, c], table[g, c + 1]
            left_panel, right_panel = own[one & 15], own[two & 15]
            left_high, right_high = flag(one >= 16), flag(two >= 16)
            pack[g, 1 + c // 2] = halves(
                left_high * turn(left_panel) + (1.0 - left_high) * left_panel,
                right_high * right_panel + (1.0 - right_high) * turn(right_panel),
            )
        return carry

    lax.fori_loop(0, len(offs), pack_group, 0)
    pl.semaphore_wait(barrier, len(partners))

    copies = []
    for g in ORDER:
        copies.append(pltpu.make_async_remote_copy(
            src_ref=pack.at[g], dst_ref=recv.at[pl.ds(g * panels, panels)],
            send_sem=send_sem.at[g], recv_sem=recv_sem.at[g],
            device_id=device(-offs[g]), device_id_type=MESH,
        ))
    pieces = (
        (1, own.at[pl.ds(6, 2)], left.at[1]),
        (1, own.at[pl.ds(10, 2)], left.at[2]),
        (1, own.at[3], left.at[0, 1]),
        (-1, own.at[pl.ds(0, 2)], right.at[0]),
        (-1, own.at[pl.ds(4, 2)], right.at[1]),
    )
    halo = [
        pltpu.make_async_remote_copy(
            src_ref=source, dst_ref=target, send_sem=halo_send.at[index], recv_sem=halo_recv.at[index],
            device_id=device(step), device_id_type=MESH,
        )
        for index, (step, source, target) in enumerate(pieces)
    ]
    for copy in halo + copies:
        copy.start()

    def far_id(row, e):
        where = rp[e, row]
        group = lax.div(where, 2)
        sender = (lax.div(row, 4) + jumps[group] + n) % n
        return sender * 4 + jnp.maximum(sr[group, where - 2 * group, sender], 0)

    def split(value):
        high = value.astype(jnp.bfloat16)
        return high, (value - high.astype(jnp.float32)).astype(jnp.bfloat16)

    def put(i, s, j, value):
        high, rest = split(value)
        gh[i, pl.ds(s * B, B), pl.ds(j * 128, 128)] = high
        gl[i, pl.ds(s * B, B), pl.ds(j * 128, 128)] = rest

    def product(left, right_high, right_rest):
        high, rest = split(left)
        both = jnp.concatenate([high, rest], axis=0)
        wide = jnp.dot(both, right_high, preferred_element_type=jnp.float32)
        return wide[:B] + wide[B:] + jnp.dot(high, right_rest, preferred_element_type=jnp.float32)

    for copy in halo:
        copy.wait()

    def narrow(i, first):
        return jnp.concatenate([own[4 * first + i], own[4 * first + 4 + i]], axis=1)

    ids = [[far_id(me * 4 + i, e) for e in range(3)] for i in range(4)]
    for i in range(4):
        for s in range(5):
            k = i + s
            if s == 2:
                for j in range(4):
                    put(i, s, j, own[4 * j + i])
                continue
            fourth = zero
            if s == 0:
                put(i, s, 0, tile(k, 1))
                put(i, s, 1, halves(tile(k, 2), zero))
            elif s == 1:
                r0, r1, r2 = turn(tile(k, 0)), turn(tile(k, 1)), turn(tile(k, 2))
                put(i, s, 0, halves(r0, r1))
                put(i, s, 1, halves(r1, r2))
            elif s == 3:
                r0, r1 = turn(tile(k, 0)), turn(tile(k, 1))
                put(i, s, 0, halves(zero, r0))
                put(i, s, 1, halves(r0, r1))
                fourth = r1
            else:
                put(i, s, 0, zero)
                put(i, s, 1, tile(k, 0))
                fourth = tile(k, 1)
            if k < 2 or k > 5:
                put(i, s, 2, halves(fourth, zero))
                put(i, s, 3, zero)
                continue
            meet = [[flag(ids[i][e] == ids[k - 2][f]) for f in range(3)] for e in range(3)]
            f2, f3 = tile(k, 2), tile(k, 3)
            g2, g3 = turn(f2), turn(f3)
            put(i, s, 2, halves(fourth, meet[0][0] * f2 + meet[0][1] * g3 + meet[0][2] * f3))
            put(i, s, 3, halves(
                meet[1][0] * g2 + meet[1][1] * f3 + meet[1][2] * g3,
                meet[2][0] * f2 + meet[2][1] * g3 + meet[2][2] * f3,
            ))
        sband[i] = product(narrow(i, 0), gh[i, pl.ds(0, 256), :], gl[i, pl.ds(0, 256), :])

    for copy in copies:
        copy.wait()

    def far_row(i, carry):
        row = me * 4 + i
        mine = [far_id(row, e) for e in range(3)]
        slots = [rp[e, row] for e in range(3)]
        groups = [lax.div(slot, 2) for slot in slots]
        columns = [(row - 2 + t + rows) % rows for t in range(5)] + mine
        for e in range(3):
            place = slots[e] - 2 * groups[e]
            theirs = [far_id(mine[e], f) for f in range(3)]
            start = groups[e] * panels

            def both_ways(spot):
                panel = recv[start + lax.div(spot, 2)]
                other = turn(panel)
                high = flag(lax.rem(spot, 2) == 1)
                return (high * other + (1.0 - high) * panel, high * panel + (1.0 - high) * other)

            def extra(candidate):
                return both_ways(2 + jnp.minimum(table[16 + groups[e], candidate], room - 1))

            far = [extra(3 * place + f) for f in range(3)]
            cross = extra(6 + place)
            diagonal = both_ways(place)
            for j in range(4):
                parts = []
                for half in range(2):
                    t = 2 * j + half
                    if t - 5 == e:
                        parts.append(diagonal[half])
                        continue
                    value = zero
                    for f in range(3):
                        value = value + flag(theirs[f] == columns[t]) * far[f][half]
                    if t >= 5:
                        distance = jnp.abs(mine[t - 5] - mine[e])
                        beside = jnp.logical_and(groups[t - 5] == groups[e], distance <= 2)
                        value = value + flag(beside) * cross[half]
                    parts.append(value)
                put(i, 5 + e, j, halves(parts[0], parts[1]))
        square = sband[i] + product(
            narrow(i, 2), gh[i, pl.ds(256, 256), :], gl[i, pl.ds(256, 256), :]
        )
        out[i] = 3.0 * square - 2.0 * product(square, gh[i], gl[i])
        return carry

    lax.fori_loop(0, 4, far_row, 0)


def step(n, offs, index, room, density, send_rows, recv_pos, table):
    groups = len(offs)
    panels = 1 + room // 2
    dma = pltpu.SemaphoreType.DMA
    smem = pl.BlockSpec(memory_space=pltpu.SMEM)
    return pl.pallas_call(
        functools.partial(kernel, n, offs, room),
        out_shape=jax.ShapeDtypeStruct(density.shape, jnp.float32),
        in_specs=[pl.BlockSpec(memory_space=pl.ANY), smem, smem, smem],
        out_specs=pl.BlockSpec(memory_space=pltpu.VMEM),
        scratch_shapes=[
            pltpu.VMEM((16, B, 128), jnp.float32),
            pltpu.VMEM((3, 2, B, 128), jnp.float32),
            pltpu.VMEM((2, 2, B, 128), jnp.float32),
            pltpu.VMEM((groups, panels, B, 128), jnp.float32),
            pltpu.VMEM((groups * panels, B, 128), jnp.float32),
            pltpu.VMEM((4, 512, 512), jnp.bfloat16),
            pltpu.VMEM((4, 512, 512), jnp.bfloat16),
            pltpu.VMEM((4, B, 512), jnp.float32),
            pltpu.SMEM((16,), jnp.int32),
            dma((4,)), dma((groups,)), dma((groups,)), dma((5,)), dma((5,)),
        ],
        compiler_params=pltpu.CompilerParams(collective_id=index, has_side_effects=True),
    )(density, send_rows, recv_pos, table)


def shards(density, send_rows, recv_pos):
    n = lax.axis_size("rows")
    offs = offset_list(n)
    send_rows = jnp.transpose(send_rows, (1, 2, 0))
    recv_pos = jnp.transpose(recv_pos, (1, 0))
    vmem, smem = (pl.BlockSpec(memory_space=space) for space in (pltpu.VMEM, pltpu.SMEM))
    table, level = pl.pallas_call(
        functools.partial(plan_kernel, n, offs),
        out_shape=(jax.ShapeDtypeStruct((32, 128), jnp.int32), jax.ShapeDtypeStruct((1,), jnp.int32)),
        in_specs=[vmem, vmem],
        out_specs=(vmem, smem),
    )(recv_pos, send_rows)
    branches = [functools.partial(step, n, offs, index, room) for index, room in enumerate(ROOMS)]
    return lax.switch(level[0], branches, density, send_rows, recv_pos, table)


def solution(mesh):
    return jax.shard_map(
        shards,
        mesh=mesh,
        in_specs=(P("rows", None, None), P(), P()),
        out_specs=P("rows", None, None),
        check_vma=False,
    )
```

```python
import functools

import jax
import jax.numpy as jnp
from jax import lax
from jax.experimental import pallas as pl
from jax.experimental.pallas import tpu as pltpu
from jax.sharding import PartitionSpec as P

MESH = pl.DeviceIdType.MESH
B = 64
ORDER = (6, 12, 5, 11, 4, 10, 3, 7, 0, 8, 1, 9, 2)
ROOMS = ((4, 4), (4, 6), (8, 8))
LONGEST = (2, 9)


def offset_list(count_dev):
    levels = count_dev.bit_length() - 1
    forward = [2 ** (position + 1) for position in range(levels - 1)]
    backward = [-(2 ** (position + 1)) for position in range(levels - 2)]
    return forward + backward


def flag(condition):
    return jnp.where(condition, 1.0, 0.0).astype(jnp.float32)


def plan_kernel(n, offs, rp, sr, table, level):
    me = lax.axis_index("rows")
    lanes = rp.shape[1]
    per = lanes // n
    row_lane = lax.broadcasted_iota(jnp.int32, (8, lanes), 1) & (per - 1)
    lists = jnp.concatenate([rp[...], jnp.zeros((5, lanes), jnp.int32)], axis=0).astype(jnp.float32)
    spread = jnp.concatenate(
        [jnp.where(row_lane == i, lists, 0.0) for i in range(per)], axis=0
    ).astype(jnp.bfloat16)
    fold = jnp.where(
        lax.broadcasted_iota(jnp.int32, (lanes, n), 0) // per == lax.broadcasted_iota(jnp.int32, (lanes, n), 1),
        1.0, 0.0,
    ).astype(jnp.bfloat16)
    picks = jnp.dot(spread, fold, preferred_element_type=jnp.float32).astype(jnp.int32)

    lane = lax.broadcasted_iota(jnp.int32, (8, n), 1)
    sub = lax.broadcasted_iota(jnp.int32, (8, n), 0)
    small_lane = lax.broadcasted_iota(jnp.int32, (8, 128), 1)
    small_sub = lax.broadcasted_iota(jnp.int32, (8, 128), 0)

    def spread_row(value, row):
        return jnp.broadcast_to(value[row:row + 1], (8, n))

    sent, bases = [], []
    for g, off in enumerate(offs):
        turned = pltpu.roll(jnp.concatenate([jnp.maximum(sr[g], 0)] * 4, axis=0), (-off) % n, 1)
        sent.append([spread_row(turned, p) for p in range(2)])
        bases.append(((lane + (off + n)) & (n - 1)) * per)
    blocks = [picks[8 * i:8 * i + 8] for i in range(per)]
    ids = [jnp.zeros((8, n), jnp.int32) for _ in range(per)]
    for g in range(len(offs)):
        for p in range(2):
            name = bases[g] + sent[g][p]
            ids = [jnp.where(block == 2 * g + p, name, known) for block, known in zip(blocks, ids)]
    id_rows = [[spread_row(ids[i], e) for e in range(3)] for i in range(per)]
    marks = []
    for block in blocks:
        bits = jnp.where(sub < 3, 1 << block, 0)
        marks.append(spread_row(bits, 0) | spread_row(bits, 1) | spread_row(bits, 2))
    edges = [lane * per + (i - 2) for i in range(per)]
    all_ids = jnp.concatenate(ids, axis=0)

    most = [jnp.zeros((8, n), jnp.int32)] * 2
    for g, off in enumerate(offs):
        moved = pltpu.roll(all_ids, (-off) % n, 1)
        parts = []
        for p in range(2):
            far = moved[0:8]
            for i in range(1, per):
                far = jnp.where(sent[g][p] == i, moved[8 * i:8 * i + 8], far)
            parts.append(far)
        far = jnp.where(sub < 3, parts[0], pltpu.roll(parts[1], 3, 0))
        place = 2 * g + jnp.where(sub < 3, 0, 1)
        need = jnp.zeros((8, n), jnp.bool_)
        both = jnp.zeros((8, n), jnp.int32)
        for i in range(per):
            meets = ((far - edges[i]) & (lanes - 1)) <= 4
            for e in range(3):
                meets = meets | (far == id_rows[i][e])
            need = need | (meets & (((marks[i] >> place) & 1) == 1))
            both = both | jnp.where(((marks[i] >> (2 * g)) & 3) == 3, 1, 0)
        delta = sent[g][1] - sent[g][0]
        cross = jnp.where(jnp.abs(delta) <= 2, both, 0)
        need = jnp.where(sub < 6, jnp.where(need, 1, 0), cross)
        rank = need
        for step in (1, 2, 4):
            rank = rank + jnp.where(sub >= step, pltpu.roll(rank, step, 0), 0)
        kind = 0 if g in LONGEST else 1
        most[kind] = jnp.maximum(most[kind], rank)
        rank = (rank - need) * need
        local = jnp.where((sub < 3) | (sub == 6), sent[g][0], sent[g][1])
        which = jnp.where(sub < 3, sub + 5, jnp.where(sub < 6, sub + 2, jnp.where(sub == 6, 2 + delta, 2 - delta)))
        code = (which & 1) * 16 + (which >> 1) * 4 + local
        mine = jnp.sum(jnp.where(lane == me, rank, 0), axis=1, keepdims=True)
        table[pl.ds(16 + g, 1), :] = jnp.sum(
            jnp.where(small_lane == small_sub, mine, 0), axis=0, keepdims=True
        )
        packed = jnp.where(need == 1, rank * 32 + code, 8 * 32)
        target = (me - off + n) & (n - 1)
        theirs = jnp.sum(jnp.where(lane == target, packed, 0), axis=1, keepdims=True)
        table[pl.ds(g, 1), :] = jnp.sum(
            jnp.where(small_lane == (theirs >> 5), theirs & 31, 0), axis=0, keepdims=True
        )
    longest, other = jnp.max(most[0]), jnp.max(most[1])
    level[0] = sum(
        jnp.where((longest > rooms[0]) | (other > rooms[1]), 1, 0) for rooms in ROOMS[:-1]
    )


def kernel(
    n, offs, rooms, x_hbm, sr_any, rp_any, table_any, out,
    own, left, right, pack, mixed, recv, gh, gl, sband, jumps, sr, rp, table, spots, meets,
    own_sem, list_sem, send_sem, recv_sem, halo_send, halo_recv,
):
    me = lax.axis_index("rows")
    rows = n * 4
    room = max(rooms)
    panels = 1 + room // 2

    def device(step):
        return {"rows": lax.rem(me + step + n, n)}

    barrier = pltpu.get_barrier_semaphore()
    partners = sorted(set(offs) | set(-o for o in offs if o * 2 != n) | {1, -1})
    for step in partners:
        pl.semaphore_signal(barrier, inc=1, device_id=device(step), device_id_type=MESH)

    loads = [
        pltpu.make_async_copy(x_hbm.at[:, :, pl.ds(128 * j, 128)], own.at[pl.ds(4 * j, 4)], own_sem.at[j])
        for j in range(4)
    ]
    lists = [
        pltpu.make_async_copy(source, target, list_sem.at[index])
        for index, (source, target) in enumerate(((sr_any, sr), (rp_any, rp), (table_any, table)))
    ]
    for load in lists + loads:
        load.start()
    for index, value in enumerate(offs):
        jumps[index] = value
    lane = lax.broadcasted_iota(jnp.int32, (B, 128), 1)
    low = lane < B
    for load in lists + loads:
        load.wait()

    def tile(k, j):
        if k < 2:
            return left[{(0, 1): 0, (1, 1): 1, (1, 2): 2, (0, 2): 3, (1, 0): 3}[k, j]]
        return right[2 * j + k - 6] if k > 5 else own[4 * j + k - 2]

    def turn(panel):
        return pltpu.roll(panel, B, 1)

    zero = jnp.zeros((B, 128), jnp.float32)

    def halves(first, second):
        return jnp.where(low, first, second)

    def pack_group(g, carry):
        first = jnp.maximum(sr[g, 0, me], 0)
        second = jnp.maximum(sr[g, 1, me], 0)
        pack[g, 0] = halves(own[4 + first], turn(own[4 + second]))
        for c in range(0, room, 2):
            one, two = table[g, c], table[g, c + 1]
            left_panel, right_panel = own[one & 15], own[two & 15]
            left_high, right_high = flag(one >= 16), flag(two >= 16)
            pack[g, 1 + c // 2] = halves(
                left_high * turn(left_panel) + (1.0 - left_high) * left_panel,
                right_high * right_panel + (1.0 - right_high) * turn(right_panel),
            )
        return carry

    lax.fori_loop(0, len(offs), pack_group, 0)
    mixed[...] = halves(own[10], own[3])
    pl.semaphore_wait(barrier, len(partners))

    copies = []
    for g in ORDER:
        held = 1 + rooms[0 if g in LONGEST else 1] // 2
        copies.append(pltpu.make_async_remote_copy(
            src_ref=pack.at[g, pl.ds(0, held)], dst_ref=recv.at[pl.ds(g * panels, held)],
            send_sem=send_sem.at[g], recv_sem=recv_sem.at[g],
            device_id=device(-offs[g]), device_id_type=MESH,
        ))
    pieces = (
        (1, own.at[pl.ds(6, 2)], left.at[pl.ds(0, 2)]),
        (1, own.at[11], left.at[2]),
        (1, mixed, left.at[3]),
        (-1, own.at[pl.ds(0, 2)], right.at[pl.ds(0, 2)]),
        (-1, own.at[pl.ds(4, 2)], right.at[pl.ds(2, 2)]),
    )
    halo = [
        pltpu.make_async_remote_copy(
            src_ref=source, dst_ref=target, send_sem=halo_send.at[index], recv_sem=halo_recv.at[index],
            device_id=device(step), device_id_type=MESH,
        )
        for index, (step, source, target) in enumerate(pieces)
    ]
    for copy in halo + copies:
        copy.start()

    def far_id(row, e):
        where = rp[e, row]
        group = lax.div(where, 2)
        sender = (lax.div(row, 4) + jumps[group] + n) % n
        return sender * 4 + jnp.maximum(sr[group, where - 2 * group, sender], 0)

    def split(value):
        high = value.astype(jnp.bfloat16)
        return high, (value - high.astype(jnp.float32)).astype(jnp.bfloat16)

    def put(i, s, j, value):
        high, rest = split(value)
        gh[i, pl.ds(s * B, B), pl.ds(j * 128, 128)] = high
        gl[i, pl.ds(s * B, B), pl.ds(j * 128, 128)] = rest

    def product(left, right_high, right_rest):
        high, rest = split(left)
        both = jnp.concatenate([high, rest], axis=0)
        wide = jnp.dot(both, right_high, preferred_element_type=jnp.float32)
        return wide[:B] + wide[B:] + jnp.dot(high, right_rest, preferred_element_type=jnp.float32)

    for copy in halo:
        copy.wait()

    def narrow(i, first):
        return jnp.concatenate([own[4 * first + i], own[4 * first + 4 + i]], axis=1)

    ids = [[far_id(me * 4 + i, e) for e in range(3)] for i in range(4)]
    for i in range(4):
        for s in range(5):
            k = i + s
            if s == 2:
                for j in range(4):
                    put(i, s, j, own[4 * j + i])
                continue
            fourth = zero
            if s == 0:
                put(i, s, 0, tile(k, 1))
                put(i, s, 1, halves(tile(k, 2), zero))
            elif s == 1:
                r0, r1, r2 = turn(tile(k, 0)), turn(tile(k, 1)), turn(tile(k, 2))
                put(i, s, 0, halves(r0, r1))
                put(i, s, 1, halves(r1, r2))
            elif s == 3:
                r0, r1 = turn(tile(k, 0)), turn(tile(k, 1))
                put(i, s, 0, halves(zero, r0))
                put(i, s, 1, halves(r0, r1))
                fourth = r1
            else:
                put(i, s, 0, zero)
                put(i, s, 1, tile(k, 0))
                fourth = tile(k, 1)
            if k < 2 or k > 5:
                put(i, s, 2, halves(fourth, zero))
                put(i, s, 3, zero)
                continue
            meet = [[flag(ids[i][e] == ids[k - 2][f]) for f in range(3)] for e in range(3)]
            f2, f3 = tile(k, 2), tile(k, 3)
            g2, g3 = turn(f2), turn(f3)
            put(i, s, 2, halves(fourth, meet[0][0] * f2 + meet[0][1] * g3 + meet[0][2] * f3))
            put(i, s, 3, halves(
                meet[1][0] * g2 + meet[1][1] * f3 + meet[1][2] * g3,
                meet[2][0] * f2 + meet[2][1] * g3 + meet[2][2] * f3,
            ))
        sband[i] = product(narrow(i, 0), gh[i, pl.ds(0, 256), :], gl[i, pl.ds(0, 256), :])

    for i in range(4):
        row = me * 4 + i
        columns = [(row - 2 + t + rows) % rows for t in range(5)] + ids[i]
        slots = [rp[e, row] for e in range(3)]
        groups = [lax.div(slot, 2) for slot in slots]
        for e in range(3):
            here = 3 * i + e
            place = slots[e] - 2 * groups[e]
            start = 2 * panels * groups[e]
            theirs = [far_id(ids[i][e], f) for f in range(3)]
            for f in range(3):
                spots[here, f] = start + 2 + table[16 + groups[e], 3 * place + f]
                for t in range(8):
                    meets[here, 8 * f + t] = jnp.where(theirs[f] == columns[t], 1, 0)
            spots[here, 3] = start + 2 + table[16 + groups[e], 6 + place]
            spots[here, 4] = start + place
            for t in range(5, 8):
                beside = jnp.logical_and(
                    groups[t - 5] == groups[e], jnp.abs(ids[i][t - 5] - ids[i][e]) <= 2
                )
                meets[here, 24 + t] = jnp.where(beside, 1, 0)

    for copy in copies:
        copy.wait()

    low_row = lax.broadcasted_iota(jnp.int32, (8, 128), 1) < B

    def twice(spot):
        panel = recv[lax.shift_right_logical(spot, 1)]
        other = turn(panel)
        high = flag((spot & 1) == 1)
        value = high * halves(other, panel) + (1.0 - high) * halves(panel, other)
        return value.reshape(8, 8, 128)

    for i in range(4):
        for e in range(3):
            here = 3 * i + e
            far = [twice(spots[here, f]) for f in range(3)]
            cross = twice(spots[here, 3])
            diagonal = twice(spots[here, 4])
            for j in range(4):
                value = jnp.zeros((8, 8, 128), jnp.float32)
                for c, source in enumerate(far + [cross]):
                    if c == 3 and j < 2:
                        continue
                    first = 0 if c == 3 and j == 2 else meets[here, 8 * c + 2 * j]
                    met = jnp.where(low_row, first, meets[here, 8 * c + 2 * j + 1]) == 1
                    value = jnp.where(met[None], source, value)
                if 2 * j == e + 5:
                    value = jnp.where(low_row[None], diagonal, value)
                elif 2 * j + 1 == e + 5:
                    value = jnp.where(low_row[None], value, diagonal)
                put(i, 5 + e, j, value.reshape(B, 128))
    squares = [
        sband[i] + product(narrow(i, 2), gh[i, pl.ds(256, 256), :], gl[i, pl.ds(256, 256), :])
        for i in range(4)
    ]
    for i in range(4):
        out[i] = 3.0 * squares[i] - 2.0 * product(squares[i], gh[i], gl[i])


def step(n, offs, index, rooms, density, send_rows, recv_pos, table):
    groups = len(offs)
    panels = 1 + max(rooms) // 2
    dma = pltpu.SemaphoreType.DMA
    stay = pl.BlockSpec(memory_space=pl.ANY)
    return pl.pallas_call(
        functools.partial(kernel, n, offs, rooms),
        out_shape=jax.ShapeDtypeStruct(density.shape, jnp.float32),
        in_specs=[stay] * 4,
        out_specs=pl.BlockSpec(memory_space=pltpu.VMEM),
        scratch_shapes=[
            pltpu.VMEM((16, B, 128), jnp.float32),
            pltpu.VMEM((4, B, 128), jnp.float32),
            pltpu.VMEM((4, B, 128), jnp.float32),
            pltpu.VMEM((groups, panels, B, 128), jnp.float32),
            pltpu.VMEM((B, 128), jnp.float32),
            pltpu.VMEM((groups * panels, B, 128), jnp.float32),
            pltpu.VMEM((4, 512, 512), jnp.bfloat16),
            pltpu.VMEM((4, 512, 512), jnp.bfloat16),
            pltpu.VMEM((4, B, 512), jnp.float32),
            pltpu.SMEM((16,), jnp.int32),
            pltpu.SMEM(send_rows.shape, jnp.int32),
            pltpu.SMEM(recv_pos.shape, jnp.int32),
            pltpu.SMEM(table.shape, jnp.int32),
            pltpu.SMEM((12, 8), jnp.int32),
            pltpu.SMEM((12, 32), jnp.int32),
            dma((4,)), dma((3,)), dma((groups,)), dma((groups,)), dma((5,)), dma((5,)),
        ],
        compiler_params=pltpu.CompilerParams(collective_id=index, has_side_effects=True),
    )(density, send_rows, recv_pos, table)


def shards(density, send_rows, recv_pos):
    n = lax.axis_size("rows")
    offs = offset_list(n)
    send_rows = jnp.transpose(send_rows, (1, 2, 0))
    recv_pos = jnp.transpose(recv_pos, (1, 0))
    vmem, smem = (pl.BlockSpec(memory_space=space) for space in (pltpu.VMEM, pltpu.SMEM))
    table, level = pl.pallas_call(
        functools.partial(plan_kernel, n, offs),
        out_shape=(jax.ShapeDtypeStruct((32, 128), jnp.int32), jax.ShapeDtypeStruct((1,), jnp.int32)),
        in_specs=[vmem, vmem],
        out_specs=(vmem, smem),
    )(recv_pos, send_rows)
    branches = [functools.partial(step, n, offs, index, rooms) for index, rooms in enumerate(ROOMS)]
    return lax.switch(level[0], branches, density, send_rows, recv_pos, table)


def solution(mesh):
    return jax.shard_map(
        shards,
        mesh=mesh,
        in_specs=(P("rows", None, None), P(), P()),
        out_specs=P("rows", None, None),
        check_vma=False,
    )
```

```python
import functools

import jax
import jax.numpy as jnp
from jax import lax
from jax.experimental import pallas as pl
from jax.experimental.pallas import tpu as pltpu
from jax.sharding import PartitionSpec as P

MESH = pl.DeviceIdType.MESH
B = 64
ORDER = (6, 12, 5, 11, 4, 10, 3, 7, 0, 8, 1, 9, 2)
ROOMS = (4, 5, 8)


def offset_list(count_dev):
    levels = count_dev.bit_length() - 1
    forward = [2 ** (position + 1) for position in range(levels - 1)]
    backward = [-(2 ** (position + 1)) for position in range(levels - 2)]
    return forward + backward


def flag(condition):
    return jnp.where(condition, 1.0, 0.0).astype(jnp.float32)


def plan_kernel(n, offs, rp, sr, table, level):
    me = lax.axis_index("rows")
    lanes = rp.shape[1]
    per = lanes // n
    row_lane = lax.broadcasted_iota(jnp.int32, (8, lanes), 1) & (per - 1)
    lists = jnp.concatenate([rp[...], jnp.zeros((5, lanes), jnp.int32)], axis=0).astype(jnp.float32)
    spread = jnp.concatenate(
        [jnp.where(row_lane == i, lists, 0.0) for i in range(per)], axis=0
    ).astype(jnp.bfloat16)
    fold = jnp.where(
        lax.broadcasted_iota(jnp.int32, (lanes, n), 0) // per == lax.broadcasted_iota(jnp.int32, (lanes, n), 1),
        1.0, 0.0,
    ).astype(jnp.bfloat16)
    picks = jnp.dot(spread, fold, preferred_element_type=jnp.float32).astype(jnp.int32)

    lane = lax.broadcasted_iota(jnp.int32, (8, n), 1)
    sub = lax.broadcasted_iota(jnp.int32, (8, n), 0)
    small_lane = lax.broadcasted_iota(jnp.int32, (8, 128), 1)
    small_sub = lax.broadcasted_iota(jnp.int32, (8, 128), 0)

    def spread_row(value, row):
        return jnp.broadcast_to(value[row:row + 1], (8, n))

    sent, bases = [], []
    for g, off in enumerate(offs):
        turned = pltpu.roll(jnp.concatenate([jnp.maximum(sr[g], 0)] * 4, axis=0), (-off) % n, 1)
        sent.append([spread_row(turned, p) for p in range(2)])
        bases.append(((lane + (off + n)) & (n - 1)) * per)
    blocks = [picks[8 * i:8 * i + 8] for i in range(per)]
    ids = [jnp.zeros((8, n), jnp.int32) for _ in range(per)]
    for g in range(len(offs)):
        for p in range(2):
            name = bases[g] + sent[g][p]
            ids = [jnp.where(block == 2 * g + p, name, known) for block, known in zip(blocks, ids)]
    id_rows = [[spread_row(ids[i], e) for e in range(3)] for i in range(per)]
    marks = []
    for block in blocks:
        bits = jnp.where(sub < 3, 1 << block, 0)
        marks.append(spread_row(bits, 0) | spread_row(bits, 1) | spread_row(bits, 2))
    edges = [lane * per + (i - 2) for i in range(per)]
    all_ids = jnp.concatenate(ids, axis=0)

    most = jnp.zeros((8, n), jnp.int32)
    for g, off in enumerate(offs):
        moved = pltpu.roll(all_ids, (-off) % n, 1)
        parts = []
        for p in range(2):
            far = moved[0:8]
            for i in range(1, per):
                far = jnp.where(sent[g][p] == i, moved[8 * i:8 * i + 8], far)
            parts.append(far)
        far = jnp.where(sub < 3, parts[0], pltpu.roll(parts[1], 3, 0))
        place = 2 * g + jnp.where(sub < 3, 0, 1)
        need = jnp.zeros((8, n), jnp.bool_)
        both = jnp.zeros((8, n), jnp.int32)
        for i in range(per):
            meets = ((far - edges[i]) & (lanes - 1)) <= 4
            for e in range(3):
                meets = meets | (far == id_rows[i][e])
            need = need | (meets & (((marks[i] >> place) & 1) == 1))
            both = both | jnp.where(((marks[i] >> (2 * g)) & 3) == 3, 1, 0)
        delta = sent[g][1] - sent[g][0]
        cross = jnp.where(jnp.abs(delta) <= 2, both, 0)
        need = jnp.where(sub < 6, jnp.where(need, 1, 0), cross)
        rank = need
        for step in (1, 2, 4):
            rank = rank + jnp.where(sub >= step, pltpu.roll(rank, step, 0), 0)
        most = jnp.maximum(most, rank)
        rank = (rank - need) * need
        local = jnp.where((sub < 3) | (sub == 6), sent[g][0], sent[g][1])
        which = jnp.where(sub < 3, sub + 5, jnp.where(sub < 6, sub + 2, jnp.where(sub == 6, 2 + delta, 2 - delta)))
        code = (which & 1) * 16 + (which >> 1) * 4 + local
        mine = jnp.sum(jnp.where(lane == me, rank, 0), axis=1, keepdims=True)
        table[pl.ds(16 + g, 1), :] = jnp.sum(
            jnp.where(small_lane == small_sub, mine, 0), axis=0, keepdims=True
        )
        packed = jnp.where(need == 1, rank * 32 + code, 8 * 32)
        target = (me - off + n) & (n - 1)
        theirs = jnp.sum(jnp.where(lane == target, packed, 0), axis=1, keepdims=True)
        table[pl.ds(g, 1), :] = jnp.sum(
            jnp.where(small_lane == (theirs >> 5), theirs & 31, 0), axis=0, keepdims=True
        )
    biggest = jnp.max(most)
    level[0] = sum(jnp.where(biggest > room, 1, 0) for room in ROOMS[:-1])


def kernel(
    n, offs, room, x_hbm, sr_any, rp_any, table_any, out,
    own, left, right, pack, mixed, recv, gh, gl, sband, jumps, sr, rp, table, spots, meets,
    own_sem, list_sem, send_sem, recv_sem, halo_send, halo_recv,
):
    me = lax.axis_index("rows")
    rows = n * 4
    size = 2 + room

    def device(step):
        return {"rows": lax.rem(me + step + n, n)}

    barrier = pltpu.get_barrier_semaphore()
    partners = sorted(set(offs) | set(-o for o in offs if o * 2 != n) | {1, -1})
    for step in partners:
        pl.semaphore_signal(barrier, inc=1, device_id=device(step), device_id_type=MESH)

    loads = [
        pltpu.make_async_copy(x_hbm.at[:, :, pl.ds(128 * j, 128)], own.at[pl.ds(4 * j, 4)], own_sem.at[j])
        for j in range(4)
    ]
    lists = [
        pltpu.make_async_copy(source, target, list_sem.at[index])
        for index, (source, target) in enumerate(((sr_any, sr), (rp_any, rp), (table_any, table)))
    ]
    for load in lists + loads:
        load.start()
    for index, value in enumerate(offs):
        jumps[index] = value
    lane = lax.broadcasted_iota(jnp.int32, (B, 128), 1)
    low = lane < B
    for load in lists + loads:
        load.wait()

    def tile(k, j):
        if k < 2:
            return left[{(0, 1): 0, (1, 1): 1, (1, 2): 2, (0, 2): 3, (1, 0): 3}[k, j]]
        return right[2 * j + k - 6] if k > 5 else own[4 * j + k - 2]

    def turn(panel):
        return pltpu.roll(panel, B, 1)

    zero = jnp.zeros((B, 128), jnp.float32)

    def halves(first, second):
        return jnp.where(low, first, second)

    def folded(panel, high):
        other = turn(panel)
        left_block = jnp.where(low[:32], panel[:32], other[32:])
        right_block = jnp.where(low[:32], other[:32], panel[32:])
        return high * right_block + (1.0 - high) * left_block

    def pack_group(g, carry):
        for p in range(2):
            pack[g, p] = folded(own[4 + jnp.maximum(sr[g, p, me], 0)], 0.0)
        for c in range(room):
            code = table[g, c]
            pack[g, 2 + c] = folded(own[code & 15], flag(code >= 16))
        return carry

    lax.fori_loop(0, len(offs), pack_group, 0)
    mixed[...] = halves(own[10], own[3])
    pl.semaphore_wait(barrier, len(partners))

    copies = []
    for g in ORDER:
        copies.append(pltpu.make_async_remote_copy(
            src_ref=pack.at[g], dst_ref=recv.at[pl.ds(g * size, size)],
            send_sem=send_sem.at[g], recv_sem=recv_sem.at[g],
            device_id=device(-offs[g]), device_id_type=MESH,
        ))
    pieces = (
        (1, own.at[pl.ds(6, 2)], left.at[pl.ds(0, 2)]),
        (1, own.at[11], left.at[2]),
        (1, mixed, left.at[3]),
        (-1, own.at[pl.ds(0, 2)], right.at[pl.ds(0, 2)]),
        (-1, own.at[pl.ds(4, 2)], right.at[pl.ds(2, 2)]),
    )
    halo = [
        pltpu.make_async_remote_copy(
            src_ref=source, dst_ref=target, send_sem=halo_send.at[index], recv_sem=halo_recv.at[index],
            device_id=device(step), device_id_type=MESH,
        )
        for index, (step, source, target) in enumerate(pieces)
    ]
    for copy in halo + copies:
        copy.start()

    def far_id(row, e):
        where = rp[e, row]
        group = lax.div(where, 2)
        sender = (lax.div(row, 4) + jumps[group] + n) % n
        return sender * 4 + jnp.maximum(sr[group, where - 2 * group, sender], 0)

    def split(value):
        high = value.astype(jnp.bfloat16)
        return high, (value - high.astype(jnp.float32)).astype(jnp.bfloat16)

    def put(i, s, j, value):
        high, rest = split(value)
        gh[i, pl.ds(s * B, B), pl.ds(j * 128, 128)] = high
        gl[i, pl.ds(s * B, B), pl.ds(j * 128, 128)] = rest

    def product(left, right_high, right_rest):
        high, rest = split(left)
        both = jnp.concatenate([high, rest], axis=0)
        wide = jnp.dot(both, right_high, preferred_element_type=jnp.float32)
        return wide[:B] + wide[B:] + jnp.dot(high, right_rest, preferred_element_type=jnp.float32)

    for copy in halo:
        copy.wait()

    def narrow(i, first):
        return jnp.concatenate([own[4 * first + i], own[4 * first + 4 + i]], axis=1)

    ids = [[far_id(me * 4 + i, e) for e in range(3)] for i in range(4)]
    for i in range(4):
        for s in range(5):
            k = i + s
            if s == 2:
                for j in range(4):
                    put(i, s, j, own[4 * j + i])
                continue
            fourth = zero
            if s == 0:
                put(i, s, 0, tile(k, 1))
                put(i, s, 1, halves(tile(k, 2), zero))
            elif s == 1:
                r0, r1, r2 = turn(tile(k, 0)), turn(tile(k, 1)), turn(tile(k, 2))
                put(i, s, 0, halves(r0, r1))
                put(i, s, 1, halves(r1, r2))
            elif s == 3:
                r0, r1 = turn(tile(k, 0)), turn(tile(k, 1))
                put(i, s, 0, halves(zero, r0))
                put(i, s, 1, halves(r0, r1))
                fourth = r1
            else:
                put(i, s, 0, zero)
                put(i, s, 1, tile(k, 0))
                fourth = tile(k, 1)
            if k < 2 or k > 5:
                put(i, s, 2, halves(fourth, zero))
                put(i, s, 3, zero)
                continue
            meet = [[flag(ids[i][e] == ids[k - 2][f]) for f in range(3)] for e in range(3)]
            f2, f3 = tile(k, 2), tile(k, 3)
            g2, g3 = turn(f2), turn(f3)
            put(i, s, 2, halves(fourth, meet[0][0] * f2 + meet[0][1] * g3 + meet[0][2] * f3))
            put(i, s, 3, halves(
                meet[1][0] * g2 + meet[1][1] * f3 + meet[1][2] * g3,
                meet[2][0] * f2 + meet[2][1] * g3 + meet[2][2] * f3,
            ))
        sband[i] = product(narrow(i, 0), gh[i, pl.ds(0, 256), :], gl[i, pl.ds(0, 256), :])

    for i in range(4):
        row = me * 4 + i
        columns = [(row - 2 + t + rows) % rows for t in range(5)] + ids[i]
        slots = [rp[e, row] for e in range(3)]
        groups = [lax.div(slot, 2) for slot in slots]
        for e in range(3):
            here = 3 * i + e
            place = slots[e] - 2 * groups[e]
            start = size * groups[e]
            theirs = [far_id(ids[i][e], f) for f in range(3)]
            for f in range(3):
                spots[here, f] = start + 2 + table[16 + groups[e], 3 * place + f]
                for t in range(8):
                    meets[here, 8 * f + t] = jnp.where(theirs[f] == columns[t], 1, 0)
            spots[here, 3] = start + 2 + table[16 + groups[e], 6 + place]
            spots[here, 4] = start + place
            for t in range(5, 8):
                beside = jnp.logical_and(
                    groups[t - 5] == groups[e], jnp.abs(ids[i][t - 5] - ids[i][e]) <= 2
                )
                meets[here, 24 + t] = jnp.where(beside, 1, 0)

    for copy in copies:
        copy.wait()

    low_row = lax.broadcasted_iota(jnp.int32, (8, 128), 1) < B

    def twice(spot):
        block = recv[spot]
        other = turn(block)
        return jnp.concatenate([
            jnp.where(low[:32], block, other), jnp.where(low[:32], other, block)
        ], axis=0).reshape(8, 8, 128)

    for i in range(4):
        for e in range(3):
            here = 3 * i + e
            far = [twice(spots[here, f]) for f in range(3)]
            cross = twice(spots[here, 3])
            diagonal = twice(spots[here, 4])
            for j in range(4):
                value = jnp.zeros((8, 8, 128), jnp.float32)
                for c, source in enumerate(far + [cross]):
                    if c == 3 and j < 2:
                        continue
                    first = 0 if c == 3 and j == 2 else meets[here, 8 * c + 2 * j]
                    met = jnp.where(low_row, first, meets[here, 8 * c + 2 * j + 1]) == 1
                    value = jnp.where(met[None], source, value)
                if 2 * j == e + 5:
                    value = jnp.where(low_row[None], diagonal, value)
                elif 2 * j + 1 == e + 5:
                    value = jnp.where(low_row[None], value, diagonal)
                put(i, 5 + e, j, value.reshape(B, 128))
    squares = [
        sband[i] + product(narrow(i, 2), gh[i, pl.ds(256, 256), :], gl[i, pl.ds(256, 256), :])
        for i in range(4)
    ]
    for i in range(4):
        out[i] = 3.0 * squares[i] - 2.0 * product(squares[i], gh[i], gl[i])


def step(n, offs, index, room, density, send_rows, recv_pos, table):
    groups = len(offs)
    size = 2 + room
    dma = pltpu.SemaphoreType.DMA
    stay = pl.BlockSpec(memory_space=pl.ANY)
    return pl.pallas_call(
        functools.partial(kernel, n, offs, room),
        out_shape=jax.ShapeDtypeStruct(density.shape, jnp.float32),
        in_specs=[stay] * 4,
        out_specs=pl.BlockSpec(memory_space=pltpu.VMEM),
        scratch_shapes=[
            pltpu.VMEM((16, B, 128), jnp.float32),
            pltpu.VMEM((4, B, 128), jnp.float32),
            pltpu.VMEM((4, B, 128), jnp.float32),
            pltpu.VMEM((groups, size, 32, 128), jnp.float32),
            pltpu.VMEM((B, 128), jnp.float32),
            pltpu.VMEM((groups * size, 32, 128), jnp.float32),
            pltpu.VMEM((4, 512, 512), jnp.bfloat16),
            pltpu.VMEM((4, 512, 512), jnp.bfloat16),
            pltpu.VMEM((4, B, 512), jnp.float32),
            pltpu.SMEM((16,), jnp.int32),
            pltpu.SMEM(send_rows.shape, jnp.int32),
            pltpu.SMEM(recv_pos.shape, jnp.int32),
            pltpu.SMEM(table.shape, jnp.int32),
            pltpu.SMEM((12, 8), jnp.int32),
            pltpu.SMEM((12, 32), jnp.int32),
            dma((4,)), dma((3,)), dma((groups,)), dma((groups,)), dma((5,)), dma((5,)),
        ],
        compiler_params=pltpu.CompilerParams(collective_id=index, has_side_effects=True),
    )(density, send_rows, recv_pos, table)


def shards(density, send_rows, recv_pos):
    n = lax.axis_size("rows")
    offs = offset_list(n)
    send_rows = jnp.transpose(send_rows, (1, 2, 0))
    recv_pos = jnp.transpose(recv_pos, (1, 0))
    vmem, smem = (pl.BlockSpec(memory_space=space) for space in (pltpu.VMEM, pltpu.SMEM))
    table, level = pl.pallas_call(
        functools.partial(plan_kernel, n, offs),
        out_shape=(jax.ShapeDtypeStruct((32, 128), jnp.int32), jax.ShapeDtypeStruct((1,), jnp.int32)),
        in_specs=[vmem, vmem],
        out_specs=(vmem, smem),
    )(recv_pos, send_rows)
    branches = [functools.partial(step, n, offs, index, room) for index, room in enumerate(ROOMS)]
    return lax.switch(level[0], branches, density, send_rows, recv_pos, table)


def solution(mesh):
    return jax.shard_map(
        shards,
        mesh=mesh,
        in_specs=(P("rows", None, None), P(), P()),
        out_specs=P("rows", None, None),
        check_vma=False,
    )
```

```python
import functools

import jax
import jax.numpy as jnp
from jax import lax
from jax.experimental import pallas as pl
from jax.experimental.pallas import tpu as pltpu
from jax.sharding import PartitionSpec as P

MESH = pl.DeviceIdType.MESH
B = 64
ORDER = (6, 12, 5, 11, 4, 10, 3, 7, 0, 8, 1, 9, 2)
ROOMS = (4, 5, 6, 8)


def offset_list(count_dev):
    levels = count_dev.bit_length() - 1
    forward = [2 ** (position + 1) for position in range(levels - 1)]
    backward = [-(2 ** (position + 1)) for position in range(levels - 2)]
    return forward + backward


def flag(condition):
    return jnp.where(condition, 1.0, 0.0).astype(jnp.float32)


def plan_kernel(n, offs, rp, sr, table, level):
    me = lax.axis_index("rows")
    lanes = rp.shape[1]
    per = lanes // n
    row_lane = lax.broadcasted_iota(jnp.int32, (8, lanes), 1) & (per - 1)
    lists = jnp.concatenate([rp[...], jnp.zeros((5, lanes), jnp.int32)], axis=0).astype(jnp.float32)
    spread = jnp.concatenate(
        [jnp.where(row_lane == i, lists, 0.0) for i in range(per)], axis=0
    ).astype(jnp.bfloat16)
    fold = jnp.where(
        lax.broadcasted_iota(jnp.int32, (lanes, n), 0) // per == lax.broadcasted_iota(jnp.int32, (lanes, n), 1),
        1.0, 0.0,
    ).astype(jnp.bfloat16)
    picks = jnp.dot(spread, fold, preferred_element_type=jnp.float32).astype(jnp.int32)

    lane = lax.broadcasted_iota(jnp.int32, (8, n), 1)
    sub = lax.broadcasted_iota(jnp.int32, (8, n), 0)
    small_lane = lax.broadcasted_iota(jnp.int32, (8, 128), 1)
    small_sub = lax.broadcasted_iota(jnp.int32, (8, 128), 0)

    def spread_row(value, row):
        return jnp.broadcast_to(value[row:row + 1], (8, n))

    sent, bases = [], []
    for g, off in enumerate(offs):
        turned = pltpu.roll(jnp.concatenate([jnp.maximum(sr[g], 0)] * 4, axis=0), (-off) % n, 1)
        sent.append([spread_row(turned, p) for p in range(2)])
        bases.append(((lane + (off + n)) & (n - 1)) * per)
    blocks = [picks[8 * i:8 * i + 8] for i in range(per)]
    ids = [jnp.zeros((8, n), jnp.int32) for _ in range(per)]
    for g in range(len(offs)):
        for p in range(2):
            name = bases[g] + sent[g][p]
            ids = [jnp.where(block == 2 * g + p, name, known) for block, known in zip(blocks, ids)]
    id_rows = [[spread_row(ids[i], e) for e in range(3)] for i in range(per)]
    marks = []
    for block in blocks:
        bits = jnp.where(sub < 3, 1 << block, 0)
        marks.append(spread_row(bits, 0) | spread_row(bits, 1) | spread_row(bits, 2))
    edges = [lane * per + (i - 2) for i in range(per)]
    all_ids = jnp.concatenate(ids, axis=0)

    most = jnp.zeros((8, n), jnp.int32)
    for g, off in enumerate(offs):
        moved = pltpu.roll(all_ids, (-off) % n, 1)
        parts = []
        for p in range(2):
            far = moved[0:8]
            for i in range(1, per):
                far = jnp.where(sent[g][p] == i, moved[8 * i:8 * i + 8], far)
            parts.append(far)
        far = jnp.where(sub < 3, parts[0], pltpu.roll(parts[1], 3, 0))
        place = 2 * g + jnp.where(sub < 3, 0, 1)
        need = jnp.zeros((8, n), jnp.bool_)
        both = jnp.zeros((8, n), jnp.int32)
        for i in range(per):
            meets = ((far - edges[i]) & (lanes - 1)) <= 4
            for e in range(3):
                meets = meets | (far == id_rows[i][e])
            need = need | (meets & (((marks[i] >> place) & 1) == 1))
            both = both | jnp.where(((marks[i] >> (2 * g)) & 3) == 3, 1, 0)
        delta = sent[g][1] - sent[g][0]
        cross = jnp.where(jnp.abs(delta) <= 2, both, 0)
        need = jnp.where(sub < 6, jnp.where(need, 1, 0), cross)
        rank = need
        for step in (1, 2, 4):
            rank = rank + jnp.where(sub >= step, pltpu.roll(rank, step, 0), 0)
        most = jnp.maximum(most, rank)
        rank = (rank - need) * need
        local = jnp.where((sub < 3) | (sub == 6), sent[g][0], sent[g][1])
        which = jnp.where(sub < 3, sub + 5, jnp.where(sub < 6, sub + 2, jnp.where(sub == 6, 2 + delta, 2 - delta)))
        code = (which & 1) * 16 + (which >> 1) * 4 + local
        mine = jnp.sum(jnp.where(lane == me, rank, 0), axis=1, keepdims=True)
        table[pl.ds(16 + g, 1), :] = jnp.sum(
            jnp.where(small_lane == small_sub, mine, 0), axis=0, keepdims=True
        )
        packed = jnp.where(need == 1, rank * 32 + code, 8 * 32)
        target = (me - off + n) & (n - 1)
        theirs = jnp.sum(jnp.where(lane == target, packed, 0), axis=1, keepdims=True)
        table[pl.ds(g, 1), :] = jnp.sum(
            jnp.where(small_lane == (theirs >> 5), theirs & 31, 0), axis=0, keepdims=True
        )
    biggest = jnp.max(most)
    level[0] = sum(jnp.where(biggest > room, 1, 0) for room in ROOMS[:-1])


def kernel(
    n, offs, room, x_hbm, sr_any, rp_any, table_any, out,
    own, left, right, pack, mixed, recv, gh, gl, sband, jumps, sr, rp, table, spots, meets,
    own_sem, list_sem, send_sem, recv_sem, halo_send, halo_recv,
):
    me = lax.axis_index("rows")
    rows = n * 4
    size = 2 + room

    def device(step):
        return {"rows": lax.rem(me + step + n, n)}

    barrier = pltpu.get_barrier_semaphore()
    partners = sorted(set(offs) | set(-o for o in offs if o * 2 != n) | {1, -1})
    for step in partners:
        pl.semaphore_signal(barrier, inc=1, device_id=device(step), device_id_type=MESH)

    loads = [
        pltpu.make_async_copy(x_hbm.at[:, :, pl.ds(128 * j, 128)], own.at[pl.ds(4 * j, 4)], own_sem.at[j])
        for j in range(4)
    ]
    lists = [
        pltpu.make_async_copy(source, target, list_sem.at[index])
        for index, (source, target) in enumerate(((sr_any, sr), (rp_any, rp), (table_any, table)))
    ]
    for load in lists + loads:
        load.start()
    for index, value in enumerate(offs):
        jumps[index] = value
    lane = lax.broadcasted_iota(jnp.int32, (B, 128), 1)
    low = lane < B
    for load in lists + loads:
        load.wait()

    def tile(k, j):
        if k < 2:
            return left[{(0, 1): 0, (1, 1): 1, (1, 2): 2, (0, 2): 3, (1, 0): 3}[k, j]]
        return right[2 * j + k - 6] if k > 5 else own[4 * j + k - 2]

    def turn(panel):
        return pltpu.roll(panel, B, 1)

    zero = jnp.zeros((B, 128), jnp.float32)

    def halves(first, second):
        return jnp.where(low, first, second)

    def folded(panel, high):
        other = turn(panel)
        left_block = jnp.where(low[:32], panel[:32], other[32:])
        right_block = jnp.where(low[:32], other[:32], panel[32:])
        return high * right_block + (1.0 - high) * left_block

    def pack_group(g, carry):
        for p in range(2):
            pack[g, p] = folded(own[4 + jnp.maximum(sr[g, p, me], 0)], 0.0)
        for c in range(room):
            code = table[g, c]
            pack[g, 2 + c] = folded(own[code & 15], flag(code >= 16))
        return carry

    lax.fori_loop(0, len(offs), pack_group, 0)
    mixed[...] = halves(own[10], own[3])
    pl.semaphore_wait(barrier, len(partners))

    copies = []
    for g in ORDER:
        copies.append(pltpu.make_async_remote_copy(
            src_ref=pack.at[g], dst_ref=recv.at[pl.ds(g * size, size)],
            send_sem=send_sem.at[g], recv_sem=recv_sem.at[g],
            device_id=device(-offs[g]), device_id_type=MESH,
        ))
    pieces = (
        (1, own.at[pl.ds(6, 2)], left.at[pl.ds(0, 2)]),
        (1, own.at[11], left.at[2]),
        (1, mixed, left.at[3]),
        (-1, own.at[pl.ds(0, 2)], right.at[pl.ds(0, 2)]),
        (-1, own.at[pl.ds(4, 2)], right.at[pl.ds(2, 2)]),
    )
    halo = [
        pltpu.make_async_remote_copy(
            src_ref=source, dst_ref=target, send_sem=halo_send.at[index], recv_sem=halo_recv.at[index],
            device_id=device(step), device_id_type=MESH,
        )
        for index, (step, source, target) in enumerate(pieces)
    ]
    for copy in halo + copies:
        copy.start()

    def far_id(row, e):
        where = rp[e, row]
        group = lax.div(where, 2)
        sender = (lax.div(row, 4) + jumps[group] + n) % n
        return sender * 4 + jnp.maximum(sr[group, where - 2 * group, sender], 0)

    def split(value):
        high = value.astype(jnp.bfloat16)
        return high, (value - high.astype(jnp.float32)).astype(jnp.bfloat16)

    def put(i, s, j, value):
        high, rest = split(value)
        gh[i, pl.ds(s * B, B), pl.ds(j * 128, 128)] = high
        gl[i, pl.ds(s * B, B), pl.ds(j * 128, 128)] = rest

    def product(left, right_high, right_rest):
        high, rest = split(left)
        both = jnp.concatenate([high, rest], axis=0)
        wide = jnp.dot(both, right_high, preferred_element_type=jnp.float32)
        return wide[:B] + wide[B:] + jnp.dot(high, right_rest, preferred_element_type=jnp.float32)

    for copy in halo:
        copy.wait()

    def narrow(i, first):
        return jnp.concatenate([own[4 * first + i], own[4 * first + 4 + i]], axis=1)

    ids = [[far_id(me * 4 + i, e) for e in range(3)] for i in range(4)]
    for i in range(4):
        for s in range(5):
            k = i + s
            if s == 2:
                for j in range(4):
                    put(i, s, j, own[4 * j + i])
                continue
            fourth = zero
            if s == 0:
                put(i, s, 0, tile(k, 1))
                put(i, s, 1, halves(tile(k, 2), zero))
            elif s == 1:
                r0, r1, r2 = turn(tile(k, 0)), turn(tile(k, 1)), turn(tile(k, 2))
                put(i, s, 0, halves(r0, r1))
                put(i, s, 1, halves(r1, r2))
            elif s == 3:
                r0, r1 = turn(tile(k, 0)), turn(tile(k, 1))
                put(i, s, 0, halves(zero, r0))
                put(i, s, 1, halves(r0, r1))
                fourth = r1
            else:
                put(i, s, 0, zero)
                put(i, s, 1, tile(k, 0))
                fourth = tile(k, 1)
            if k < 2 or k > 5:
                put(i, s, 2, halves(fourth, zero))
                put(i, s, 3, zero)
                continue
            meet = [[flag(ids[i][e] == ids[k - 2][f]) for f in range(3)] for e in range(3)]
            f2, f3 = tile(k, 2), tile(k, 3)
            g2, g3 = turn(f2), turn(f3)
            put(i, s, 2, halves(fourth, meet[0][0] * f2 + meet[0][1] * g3 + meet[0][2] * f3))
            put(i, s, 3, halves(
                meet[1][0] * g2 + meet[1][1] * f3 + meet[1][2] * g3,
                meet[2][0] * f2 + meet[2][1] * g3 + meet[2][2] * f3,
            ))
        sband[i] = product(narrow(i, 0), gh[i, pl.ds(0, 256), :], gl[i, pl.ds(0, 256), :])

    for i in range(4):
        row = me * 4 + i
        columns = [(row - 2 + t + rows) % rows for t in range(5)] + ids[i]
        slots = [rp[e, row] for e in range(3)]
        groups = [lax.div(slot, 2) for slot in slots]
        for e in range(3):
            here = 3 * i + e
            place = slots[e] - 2 * groups[e]
            start = size * groups[e]
            theirs = [far_id(ids[i][e], f) for f in range(3)]
            for f in range(3):
                spots[here, f] = start + 2 + table[16 + groups[e], 3 * place + f]
                for t in range(8):
                    meets[here, 8 * f + t] = jnp.where(theirs[f] == columns[t], 1, 0)
            spots[here, 3] = start + 2 + table[16 + groups[e], 6 + place]
            spots[here, 4] = start + place
            for t in range(5, 8):
                beside = jnp.logical_and(
                    groups[t - 5] == groups[e], jnp.abs(ids[i][t - 5] - ids[i][e]) <= 2
                )
                meets[here, 24 + t] = jnp.where(beside, 1, 0)

    for copy in copies:
        copy.wait()

    low_row = lax.broadcasted_iota(jnp.int32, (8, 128), 1) < B

    def twice(spot):
        block = recv[spot]
        other = turn(block)
        return jnp.concatenate([
            jnp.where(low[:32], block, other), jnp.where(low[:32], other, block)
        ], axis=0).reshape(8, 8, 128)

    for i in range(4):
        for e in range(3):
            here = 3 * i + e
            far = [twice(spots[here, f]) for f in range(3)]
            cross = twice(spots[here, 3])
            diagonal = twice(spots[here, 4])
            for j in range(4):
                value = jnp.zeros((8, 8, 128), jnp.float32)
                for c, source in enumerate(far + [cross]):
                    if c == 3 and j < 2:
                        continue
                    first = 0 if c == 3 and j == 2 else meets[here, 8 * c + 2 * j]
                    met = jnp.where(low_row, first, meets[here, 8 * c + 2 * j + 1]) == 1
                    value = jnp.where(met[None], source, value)
                if 2 * j == e + 5:
                    value = jnp.where(low_row[None], diagonal, value)
                elif 2 * j + 1 == e + 5:
                    value = jnp.where(low_row[None], value, diagonal)
                put(i, 5 + e, j, value.reshape(B, 128))
    squares = [
        sband[i] + product(narrow(i, 2), gh[i, pl.ds(256, 256), :], gl[i, pl.ds(256, 256), :])
        for i in range(4)
    ]
    for i in range(4):
        out[i] = 3.0 * squares[i] - 2.0 * product(squares[i], gh[i], gl[i])


def step(n, offs, index, room, density, send_rows, recv_pos, table):
    groups = len(offs)
    size = 2 + room
    dma = pltpu.SemaphoreType.DMA
    stay = pl.BlockSpec(memory_space=pl.ANY)
    return pl.pallas_call(
        functools.partial(kernel, n, offs, room),
        out_shape=jax.ShapeDtypeStruct(density.shape, jnp.float32),
        in_specs=[stay] * 4,
        out_specs=pl.BlockSpec(memory_space=pltpu.VMEM),
        scratch_shapes=[
            pltpu.VMEM((16, B, 128), jnp.float32),
            pltpu.VMEM((4, B, 128), jnp.float32),
            pltpu.VMEM((4, B, 128), jnp.float32),
            pltpu.VMEM((groups, size, 32, 128), jnp.float32),
            pltpu.VMEM((B, 128), jnp.float32),
            pltpu.VMEM((groups * size, 32, 128), jnp.float32),
            pltpu.VMEM((4, 512, 512), jnp.bfloat16),
            pltpu.VMEM((4, 512, 512), jnp.bfloat16),
            pltpu.VMEM((4, B, 512), jnp.float32),
            pltpu.SMEM((16,), jnp.int32),
            pltpu.SMEM(send_rows.shape, jnp.int32),
            pltpu.SMEM(recv_pos.shape, jnp.int32),
            pltpu.SMEM(table.shape, jnp.int32),
            pltpu.SMEM((12, 8), jnp.int32),
            pltpu.SMEM((12, 32), jnp.int32),
            dma((4,)), dma((3,)), dma((groups,)), dma((groups,)), dma((5,)), dma((5,)),
        ],
        compiler_params=pltpu.CompilerParams(collective_id=index, has_side_effects=True),
    )(density, send_rows, recv_pos, table)


def shards(density, send_rows, recv_pos):
    n = lax.axis_size("rows")
    offs = offset_list(n)
    send_rows = jnp.transpose(send_rows, (1, 2, 0))
    recv_pos = jnp.transpose(recv_pos, (1, 0))
    vmem, smem = (pl.BlockSpec(memory_space=space) for space in (pltpu.VMEM, pltpu.SMEM))
    table, level = pl.pallas_call(
        functools.partial(plan_kernel, n, offs),
        out_shape=(jax.ShapeDtypeStruct((32, 128), jnp.int32), jax.ShapeDtypeStruct((1,), jnp.int32)),
        in_specs=[vmem, vmem],
        out_specs=(vmem, smem),
    )(recv_pos, send_rows)
    branches = [functools.partial(step, n, offs, index, room) for index, room in enumerate(ROOMS)]
    return lax.switch(level[0], branches, density, send_rows, recv_pos, table)


def solution(mesh):
    return jax.shard_map(
        shards,
        mesh=mesh,
        in_specs=(P("rows", None, None), P(), P()),
        out_specs=P("rows", None, None),
        check_vma=False,
    )
```

```python
import functools

import jax
import jax.numpy as jnp
from jax import lax
from jax.experimental import pallas as pl
from jax.experimental.pallas import tpu as pltpu
from jax.sharding import PartitionSpec as P

MESH = pl.DeviceIdType.MESH
B = 64
ORDER = (6, 12, 5, 11, 4, 10, 3, 7, 0, 8, 1, 9, 2)
ROOMS = ((4, 4), (5, 4), (4, 5), (5, 5), (6, 6), (8, 8))


def kind(off):
    return 0 if abs(off) <= 8 else 1


def offset_list(count_dev):
    levels = count_dev.bit_length() - 1
    forward = [2 ** (position + 1) for position in range(levels - 1)]
    backward = [-(2 ** (position + 1)) for position in range(levels - 2)]
    return forward + backward


def flag(condition):
    return jnp.where(condition, 1.0, 0.0).astype(jnp.float32)


def plan_kernel(n, offs, rp, sr, table, level):
    me = lax.axis_index("rows")
    lanes = rp.shape[1]
    per = lanes // n
    row_lane = lax.broadcasted_iota(jnp.int32, (8, lanes), 1) & (per - 1)
    lists = jnp.concatenate([rp[...], jnp.zeros((5, lanes), jnp.int32)], axis=0).astype(jnp.float32)
    spread = jnp.concatenate(
        [jnp.where(row_lane == i, lists, 0.0) for i in range(per)], axis=0
    ).astype(jnp.bfloat16)
    fold = jnp.where(
        lax.broadcasted_iota(jnp.int32, (lanes, n), 0) // per == lax.broadcasted_iota(jnp.int32, (lanes, n), 1),
        1.0, 0.0,
    ).astype(jnp.bfloat16)
    picks = jnp.dot(spread, fold, preferred_element_type=jnp.float32).astype(jnp.int32)

    lane = lax.broadcasted_iota(jnp.int32, (8, n), 1)
    sub = lax.broadcasted_iota(jnp.int32, (8, n), 0)
    small_lane = lax.broadcasted_iota(jnp.int32, (8, 128), 1)
    small_sub = lax.broadcasted_iota(jnp.int32, (8, 128), 0)

    def spread_row(value, row):
        return jnp.broadcast_to(value[row:row + 1], (8, n))

    sent, bases = [], []
    for g, off in enumerate(offs):
        turned = pltpu.roll(jnp.concatenate([jnp.maximum(sr[g], 0)] * 4, axis=0), (-off) % n, 1)
        sent.append([spread_row(turned, p) for p in range(2)])
        bases.append(((lane + (off + n)) & (n - 1)) * per)
    blocks = [picks[8 * i:8 * i + 8] for i in range(per)]
    ids = [jnp.zeros((8, n), jnp.int32) for _ in range(per)]
    for g in range(len(offs)):
        for p in range(2):
            name = bases[g] + sent[g][p]
            ids = [jnp.where(block == 2 * g + p, name, known) for block, known in zip(blocks, ids)]
    id_rows = [[spread_row(ids[i], e) for e in range(3)] for i in range(per)]
    marks = []
    for block in blocks:
        bits = jnp.where(sub < 3, 1 << block, 0)
        marks.append(spread_row(bits, 0) | spread_row(bits, 1) | spread_row(bits, 2))
    edges = [lane * per + (i - 2) for i in range(per)]
    all_ids = jnp.concatenate(ids, axis=0)

    most = [jnp.zeros((8, n), jnp.int32)] * 2
    for g, off in enumerate(offs):
        moved = pltpu.roll(all_ids, (-off) % n, 1)
        parts = []
        for p in range(2):
            far = moved[0:8]
            for i in range(1, per):
                far = jnp.where(sent[g][p] == i, moved[8 * i:8 * i + 8], far)
            parts.append(far)
        far = jnp.where(sub < 3, parts[0], pltpu.roll(parts[1], 3, 0))
        place = 2 * g + jnp.where(sub < 3, 0, 1)
        need = jnp.zeros((8, n), jnp.bool_)
        both = jnp.zeros((8, n), jnp.int32)
        for i in range(per):
            meets = ((far - edges[i]) & (lanes - 1)) <= 4
            for e in range(3):
                meets = meets | (far == id_rows[i][e])
            need = need | (meets & (((marks[i] >> place) & 1) == 1))
            both = both | jnp.where(((marks[i] >> (2 * g)) & 3) == 3, 1, 0)
        delta = sent[g][1] - sent[g][0]
        cross = jnp.where(jnp.abs(delta) <= 2, both, 0)
        need = jnp.where(sub < 6, jnp.where(need, 1, 0), cross)
        rank = need
        for step in (1, 2, 4):
            rank = rank + jnp.where(sub >= step, pltpu.roll(rank, step, 0), 0)
        most[kind(off)] = jnp.maximum(most[kind(off)], rank)
        rank = (rank - need) * need
        local = jnp.where((sub < 3) | (sub == 6), sent[g][0], sent[g][1])
        which = jnp.where(sub < 3, sub + 5, jnp.where(sub < 6, sub + 2, jnp.where(sub == 6, 2 + delta, 2 - delta)))
        code = (which & 1) * 16 + (which >> 1) * 4 + local
        mine = jnp.sum(jnp.where(lane == me, rank, 0), axis=1, keepdims=True)
        table[pl.ds(16 + g, 1), :] = jnp.sum(
            jnp.where(small_lane == small_sub, mine, 0), axis=0, keepdims=True
        )
        packed = jnp.where(need == 1, rank * 32 + code, 8 * 32)
        target = (me - off + n) & (n - 1)
        theirs = jnp.sum(jnp.where(lane == target, packed, 0), axis=1, keepdims=True)
        table[pl.ds(g, 1), :] = jnp.sum(
            jnp.where(small_lane == (theirs >> 5), theirs & 31, 0), axis=0, keepdims=True
        )
    near, far = jnp.max(most[0]), jnp.max(most[1])
    found = jnp.int32(len(ROOMS) - 1)
    for index in range(len(ROOMS) - 2, -1, -1):
        serves = (near <= ROOMS[index][0]) & (far <= ROOMS[index][1])
        found = jnp.where(serves, index, found)
    level[0] = found


def kernel(
    n, offs, rooms, x_hbm, sr_any, rp_any, table_any, out,
    own, left, right, pack, mixed, recv, gh, gl, sband, jumps, sr, rp, table, spots, meets,
    own_sem, list_sem, send_sem, recv_sem, halo_send, halo_recv,
):
    me = lax.axis_index("rows")
    rows = n * 4
    room = max(rooms)
    size = 2 + room

    def device(step):
        return {"rows": lax.rem(me + step + n, n)}

    barrier = pltpu.get_barrier_semaphore()
    partners = sorted(set(offs) | set(-o for o in offs if o * 2 != n) | {1, -1})
    for step in partners:
        pl.semaphore_signal(barrier, inc=1, device_id=device(step), device_id_type=MESH)

    loads = [
        pltpu.make_async_copy(x_hbm.at[:, :, pl.ds(128 * j, 128)], own.at[pl.ds(4 * j, 4)], own_sem.at[j])
        for j in range(4)
    ]
    lists = [
        pltpu.make_async_copy(source, target, list_sem.at[index])
        for index, (source, target) in enumerate(((sr_any, sr), (rp_any, rp), (table_any, table)))
    ]
    for load in lists + loads:
        load.start()
    for index, value in enumerate(offs):
        jumps[index] = value
    lane = lax.broadcasted_iota(jnp.int32, (B, 128), 1)
    low = lane < B
    for load in lists + loads:
        load.wait()

    def tile(k, j):
        if k < 2:
            return left[{(0, 1): 0, (1, 1): 1, (1, 2): 2, (0, 2): 3, (1, 0): 3}[k, j]]
        return right[2 * j + k - 6] if k > 5 else own[4 * j + k - 2]

    def turn(panel):
        return pltpu.roll(panel, B, 1)

    zero = jnp.zeros((B, 128), jnp.float32)

    def halves(first, second):
        return jnp.where(low, first, second)

    def folded(panel, high):
        other = turn(panel)
        left_block = jnp.where(low[:32], panel[:32], other[32:])
        right_block = jnp.where(low[:32], other[:32], panel[32:])
        return high * right_block + (1.0 - high) * left_block

    def pack_group(g, carry):
        for p in range(2):
            pack[g, p] = folded(own[4 + jnp.maximum(sr[g, p, me], 0)], 0.0)
        for c in range(room):
            code = table[g, c]
            pack[g, 2 + c] = folded(own[code & 15], flag(code >= 16))
        return carry

    lax.fori_loop(0, len(offs), pack_group, 0)
    mixed[...] = halves(own[10], own[3])
    pl.semaphore_wait(barrier, len(partners))

    copies = []
    for g in ORDER:
        held = 2 + rooms[kind(offs[g])]
        copies.append(pltpu.make_async_remote_copy(
            src_ref=pack.at[g, pl.ds(0, held)], dst_ref=recv.at[pl.ds(g * size, held)],
            send_sem=send_sem.at[g], recv_sem=recv_sem.at[g],
            device_id=device(-offs[g]), device_id_type=MESH,
        ))
    pieces = (
        (1, own.at[pl.ds(6, 2)], left.at[pl.ds(0, 2)]),
        (1, own.at[11], left.at[2]),
        (1, mixed, left.at[3]),
        (-1, own.at[pl.ds(0, 2)], right.at[pl.ds(0, 2)]),
        (-1, own.at[pl.ds(4, 2)], right.at[pl.ds(2, 2)]),
    )
    halo = [
        pltpu.make_async_remote_copy(
            src_ref=source, dst_ref=target, send_sem=halo_send.at[index], recv_sem=halo_recv.at[index],
            device_id=device(step), device_id_type=MESH,
        )
        for index, (step, source, target) in enumerate(pieces)
    ]
    for copy in halo + copies:
        copy.start()

    def far_id(row, e):
        where = rp[e, row]
        group = lax.div(where, 2)
        sender = (lax.div(row, 4) + jumps[group] + n) % n
        return sender * 4 + jnp.maximum(sr[group, where - 2 * group, sender], 0)

    def split(value):
        high = value.astype(jnp.bfloat16)
        return high, (value - high.astype(jnp.float32)).astype(jnp.bfloat16)

    def put(i, s, j, value):
        high, rest = split(value)
        gh[i, pl.ds(s * B, B), pl.ds(j * 128, 128)] = high
        gl[i, pl.ds(s * B, B), pl.ds(j * 128, 128)] = rest

    def product(left, right_high, right_rest):
        high, rest = split(left)
        both = jnp.concatenate([high, rest], axis=0)
        wide = jnp.dot(both, right_high, preferred_element_type=jnp.float32)
        return wide[:B] + wide[B:] + jnp.dot(high, right_rest, preferred_element_type=jnp.float32)

    for copy in halo:
        copy.wait()

    def narrow(i, first):
        return jnp.concatenate([own[4 * first + i], own[4 * first + 4 + i]], axis=1)

    ids = [[far_id(me * 4 + i, e) for e in range(3)] for i in range(4)]
    for i in range(4):
        for s in range(5):
            k = i + s
            if s == 2:
                for j in range(4):
                    put(i, s, j, own[4 * j + i])
                continue
            fourth = zero
            if s == 0:
                put(i, s, 0, tile(k, 1))
                put(i, s, 1, halves(tile(k, 2), zero))
            elif s == 1:
                r0, r1, r2 = turn(tile(k, 0)), turn(tile(k, 1)), turn(tile(k, 2))
                put(i, s, 0, halves(r0, r1))
                put(i, s, 1, halves(r1, r2))
            elif s == 3:
                r0, r1 = turn(tile(k, 0)), turn(tile(k, 1))
                put(i, s, 0, halves(zero, r0))
                put(i, s, 1, halves(r0, r1))
                fourth = r1
            else:
                put(i, s, 0, zero)
                put(i, s, 1, tile(k, 0))
                fourth = tile(k, 1)
            if k < 2 or k > 5:
                put(i, s, 2, halves(fourth, zero))
                put(i, s, 3, zero)
                continue
            meet = [[flag(ids[i][e] == ids[k - 2][f]) for f in range(3)] for e in range(3)]
            f2, f3 = tile(k, 2), tile(k, 3)
            g2, g3 = turn(f2), turn(f3)
            put(i, s, 2, halves(fourth, meet[0][0] * f2 + meet[0][1] * g3 + meet[0][2] * f3))
            put(i, s, 3, halves(
                meet[1][0] * g2 + meet[1][1] * f3 + meet[1][2] * g3,
                meet[2][0] * f2 + meet[2][1] * g3 + meet[2][2] * f3,
            ))
        sband[i] = product(narrow(i, 0), gh[i, pl.ds(0, 256), :], gl[i, pl.ds(0, 256), :])

    for i in range(4):
        row = me * 4 + i
        columns = [(row - 2 + t + rows) % rows for t in range(5)] + ids[i]
        slots = [rp[e, row] for e in range(3)]
        groups = [lax.div(slot, 2) for slot in slots]
        for e in range(3):
            here = 3 * i + e
            place = slots[e] - 2 * groups[e]
            start = size * groups[e]
            theirs = [far_id(ids[i][e], f) for f in range(3)]
            for f in range(3):
                spots[here, f] = start + 2 + table[16 + groups[e], 3 * place + f]
                for t in range(8):
                    meets[here, 8 * f + t] = jnp.where(theirs[f] == columns[t], 1, 0)
            spots[here, 3] = start + 2 + table[16 + groups[e], 6 + place]
            spots[here, 4] = start + place
            for t in range(5, 8):
                beside = jnp.logical_and(
                    groups[t - 5] == groups[e], jnp.abs(ids[i][t - 5] - ids[i][e]) <= 2
                )
                meets[here, 24 + t] = jnp.where(beside, 1, 0)

    for copy in copies:
        copy.wait()

    low_row = lax.broadcasted_iota(jnp.int32, (8, 128), 1) < B

    def twice(spot):
        block = recv[spot]
        other = turn(block)
        return jnp.concatenate([
            jnp.where(low[:32], block, other), jnp.where(low[:32], other, block)
        ], axis=0).reshape(8, 8, 128)

    for i in range(4):
        for e in range(3):
            here = 3 * i + e
            far = [twice(spots[here, f]) for f in range(3)]
            cross = twice(spots[here, 3])
            diagonal = twice(spots[here, 4])
            for j in range(4):
                value = jnp.zeros((8, 8, 128), jnp.float32)
                for c, source in enumerate(far + [cross]):
                    if c == 3 and j < 2:
                        continue
                    first = 0 if c == 3 and j == 2 else meets[here, 8 * c + 2 * j]
                    met = jnp.where(low_row, first, meets[here, 8 * c + 2 * j + 1]) == 1
                    value = jnp.where(met[None], source, value)
                if 2 * j == e + 5:
                    value = jnp.where(low_row[None], diagonal, value)
                elif 2 * j + 1 == e + 5:
                    value = jnp.where(low_row[None], value, diagonal)
                put(i, 5 + e, j, value.reshape(B, 128))
    squares = [
        sband[i] + product(narrow(i, 2), gh[i, pl.ds(256, 256), :], gl[i, pl.ds(256, 256), :])
        for i in range(4)
    ]
    for i in range(4):
        out[i] = 3.0 * squares[i] - 2.0 * product(squares[i], gh[i], gl[i])


def step(n, offs, index, rooms, density, send_rows, recv_pos, table):
    groups = len(offs)
    room = max(rooms)
    size = 2 + room
    dma = pltpu.SemaphoreType.DMA
    stay = pl.BlockSpec(memory_space=pl.ANY)
    return pl.pallas_call(
        functools.partial(kernel, n, offs, rooms),
        out_shape=jax.ShapeDtypeStruct(density.shape, jnp.float32),
        in_specs=[stay] * 4,
        out_specs=pl.BlockSpec(memory_space=pltpu.VMEM),
        scratch_shapes=[
            pltpu.VMEM((16, B, 128), jnp.float32),
            pltpu.VMEM((4, B, 128), jnp.float32),
            pltpu.VMEM((4, B, 128), jnp.float32),
            pltpu.VMEM((groups, size, 32, 128), jnp.float32),
            pltpu.VMEM((B, 128), jnp.float32),
            pltpu.VMEM((groups * size, 32, 128), jnp.float32),
            pltpu.VMEM((4, 512, 512), jnp.bfloat16),
            pltpu.VMEM((4, 512, 512), jnp.bfloat16),
            pltpu.VMEM((4, B, 512), jnp.float32),
            pltpu.SMEM((16,), jnp.int32),
            pltpu.SMEM(send_rows.shape, jnp.int32),
            pltpu.SMEM(recv_pos.shape, jnp.int32),
            pltpu.SMEM(table.shape, jnp.int32),
            pltpu.SMEM((12, 8), jnp.int32),
            pltpu.SMEM((12, 32), jnp.int32),
            dma((4,)), dma((3,)), dma((groups,)), dma((groups,)), dma((5,)), dma((5,)),
        ],
        compiler_params=pltpu.CompilerParams(collective_id=index, has_side_effects=True),
    )(density, send_rows, recv_pos, table)


def shards(density, send_rows, recv_pos):
    n = lax.axis_size("rows")
    offs = offset_list(n)
    send_rows = jnp.transpose(send_rows, (1, 2, 0))
    recv_pos = jnp.transpose(recv_pos, (1, 0))
    vmem, smem = (pl.BlockSpec(memory_space=space) for space in (pltpu.VMEM, pltpu.SMEM))
    table, level = pl.pallas_call(
        functools.partial(plan_kernel, n, offs),
        out_shape=(jax.ShapeDtypeStruct((32, 128), jnp.int32), jax.ShapeDtypeStruct((1,), jnp.int32)),
        in_specs=[vmem, vmem],
        out_specs=(vmem, smem),
    )(recv_pos, send_rows)
    branches = [functools.partial(step, n, offs, index, rooms) for index, rooms in enumerate(ROOMS)]
    return lax.switch(level[0], branches, density, send_rows, recv_pos, table)


def solution(mesh):
    return jax.shard_map(
        shards,
        mesh=mesh,
        in_specs=(P("rows", None, None), P(), P()),
        out_specs=P("rows", None, None),
        check_vma=False,
    )
```
